32 devices in a mesh: groups: 2 (over x), blk: 16 (over z, y, core).
Axes of the slice: x: 2, y: 2, z: 4, core: 2. Of those that a mesh axis runs over, the one named last changes fastest.
Arguments:
- points_in: bfloat16 [16384, 768], P(('groups', 'blk')), parts along dimension 0, may hold values from -6 to 6
- hidden_weight: bfloat16 [768, 2560], replicated, may hold values from -0.21875 to 0.21875
- output_weight: bfloat16 [2560, 768], replicated, may hold values from -0.125 to 0.125
- point_owner: int32 [16384, 1], P(('groups', 'blk')), parts along dimension 0, may hold values from 0 to 15; in each aligned block of 512 rows (0 to 511, 512 to 1023, ...) at most 64 rows name the same one
- point_node: int32 [16384], P(('groups', 'blk')), parts along dimension 0, may hold values from 0 to 31
- point_weight: int32 [16384], P(('groups', 'blk')), parts along dimension 0, may hold values from 1 to 4
- proj_weight: bfloat16 [768, 2304], replicated, may hold values from -8 to 8
- final_gain: bfloat16 [768], replicated, may hold values from 0.5 to 1.5
Outputs:
- supernodes: bfloat16 [1024, 768], P(('groups', 'blk')), parts along dimension 0
The draws below stay inside these ranges and needn't reach their ends.
There are 2 independent parts, one for each index of `groups`. The reference program is written for one: setup_inputs(seed, part) draws one part's arguments, and reference() takes and returns one part's arrays. A program takes and returns all parts, laid end to end along the dimension named above; an argument that names none is the same for every part. Nothing has to cross between parts.
Inputs may be any that keep to these rules, and one draw needn't show every extreme that they name: `point_owner`: among the 512 points of one blk index, at most 64 name the same owner, a bound that some block reaches of them.
All inputs are finite; a program needn't handle non-finite values.
Results may differ from the reference program's by a relative error of at most 0.0067.
Values may be sent and summed in bfloat16 or wider, within the bound.
A program may use at most 128 MiB of HBM per device.

```python
import math
import jax
import jax.numpy as jnp
import numpy as np
from jax import lax

D = 768
HEADS = 12
FF = 2560
P_DEV = 512
S_DEV = 32
DH = 64
OWNERS = 16
CAP = 64
POINTS = 8192
NSUP = 512
N_BLK = 16


def draw_proj_weight(key, part):
    first_key = jax.random.fold_in(key, 11)
    second_key = jax.random.fold_in(key, 23)
    base = jax.random.truncated_normal(first_key, -4.0, 4.0, (D, 3 * D), jnp.float32) * D ** (-0.5)
    query_part = base[:, :D]
    factors = jax.random.permutation(second_key, jnp.arange(HEADS, dtype=jnp.int32) % 3 + 1).astype(jnp.float32)
    column_factor = jnp.repeat(factors, DH)
    query_new = column_factor[None, :] * query_part
    base = jnp.concatenate([jnp.clip(query_new, -8.0, 8.0), base[:, D:]], axis=1)
    return base.astype(jnp.bfloat16)


def touch_ends(drawn, own_key, least, largest):
    longest = drawn.shape.index(max(drawn.shape))
    spots = []
    for shift in (0, 1):
        where = [jax.random.randint(jax.random.fold_in(own_key, axis), (), 0, length) for axis, length in enumerate(drawn.shape)]
        where[longest] = (where[longest] + shift) % drawn.shape[longest]
        spots.append(tuple(where))
    return drawn.at[spots[0]].set(least).at[spots[1]].set(largest)


def steps_of(key, shape, cuts, low, high):
    level, own = 1.0, jax.random.fold_in(key, 6)
    for position, shards_of in cuts:
        draws = jnp.exp(jax.random.uniform(jax.random.fold_in(own, position), (shards_of,), jnp.float32, low / len(cuts), high / len(cuts)))
        level = level * jnp.repeat(draws, shape[position] // shards_of).reshape([-1 if axis == position else 1 for axis in range(len(shape))])
    return level


def shared_out(stream_key, own, number, rows, number_of, top, bound, lean):
    order = jax.random.permutation(stream_key, number_of)
    heavy_load, ordinary = load_shares(number_of, rows * top, bound, lean, True), load_shares(number_of, rows * top, bound, lean, False)
    places = jnp.arange(number_of)

    def named(tallies, turn):
        used = int((tallies > 0).sum())
        fixed = max(1, used // 4)
        moved = fixed + (places - fixed + turn * (used - fixed)) % max(1, number_of - fixed)
        return jnp.zeros((number_of,), jnp.int32).at[order[jnp.where(places < fixed, places, moved)]].set(jnp.asarray(tallies, jnp.int32))

    tallies = jnp.where(number % 4 == 0, named(heavy_load, number // 4), named(ordinary, number - number // 4 - 1))
    mixed = jax.random.permutation(jax.random.fold_in(own, 3), number_of)
    donor, taker = mixed[0:number_of // 2 * 2:2], mixed[1:number_of // 2 * 2:2]
    margin = jnp.minimum(tallies[donor] - 1, bound - tallies[taker]) // 2
    margin = jnp.where((donor == order[0]) | (taker == order[0]) | (tallies[taker] == 0), 0, jnp.maximum(margin, 0))
    moved = jax.random.randint(jax.random.fold_in(own, 4), (number_of // 2,), 0, 1 << 20) % (margin + 1)
    tallies = tallies.at[donor].add(-moved).at[taker].add(moved)
    members = jnp.searchsorted(jnp.cumsum(tallies), jnp.arange(rows * top), side="right").astype(jnp.int32)
    table = members.reshape(top, rows).T
    table = table[jax.random.permutation(jax.random.fold_in(own, 1), rows)]
    turn = jax.random.randint(jax.random.fold_in(own, 2), (rows, 1), 0, top)
    return jnp.take_along_axis(table, (jnp.arange(top)[None, :] + turn) % top, axis=1)


def load_shares(amount, total, reach, skew, full):
    weights = [(1 << 20) // math.isqrt(grade ** skew) + 1 for grade in range(1, amount + 1)]
    largest = reach if full else min(reach, max(-(-total // amount), total * weights[0] // sum(weights)))
    least = 1 if total - largest >= amount - 1 else 0
    holding, surplus = [largest] + [least] * (amount - 1), total - largest - least * (amount - 1)
    while surplus > 0:
        movable = [i for i in range(1, amount) if holding[i] < largest] or [i for i in range(1, amount) if holding[i] < reach]
        whole, remaining = sum([weights[i] for i in movable]), surplus
        for i in movable:
            extra = min(reach - holding[i], max(1, remaining * weights[i] // whole), surplus)
            holding[i] = holding[i] + extra
            surplus = surplus - extra
    return np.array(holding)


def normal_values(key, extent, deviation, reach, shards=(), kind=jnp.bfloat16):
    drawn = jax.random.normal(key, extent, jnp.float32) * deviation
    if len(shards) > 0:
        drawn = steps_of(key, extent, shards, -0.22, 0.18) * drawn
    return jnp.clip(drawn, min=-reach, max=reach).astype(kind)


def setup_inputs(seed: int = 0, part: int = 0) -> dict:
    seeds = jax.random.split(jax.random.key(seed), 9)
    part_keys = jax.random.split(jax.random.fold_in(seeds[8], part), 9)
    points_in = normal_values(part_keys[0], (POINTS, D), 1.0, 6.0, ((0, 16),))
    hidden_weight = normal_values(seeds[1], (D, FF), D ** -0.5, 0.21875)
    output_weight = normal_values(seeds[2], (FF, D), FF ** -0.5, 0.125)
    point_owner_keys = jax.random.split(jax.random.fold_in(part_keys[3], 1), POINTS // P_DEV)
    point_owner_turns = jax.random.permutation(jax.random.fold_in(part_keys[3], 3), POINTS // P_DEV)
    point_owner = jax.vmap(lambda own, number: shared_out(jax.random.fold_in(part_keys[3], 2), own, number, P_DEV, OWNERS, 1, CAP, 1))(point_owner_keys, point_owner_turns).reshape((POINTS, 1))
    point_node = touch_ends(jax.random.randint(part_keys[4], (POINTS,), 0, S_DEV), jax.random.fold_in(part_keys[4], 1), 0, S_DEV - 1).astype(jnp.int32)
    point_weight = touch_ends(jax.random.randint(part_keys[5], (POINTS,), 1, 5), jax.random.fold_in(part_keys[5], 1), 1, 4).astype(jnp.int32)
    proj_weight = draw_proj_weight(jax.random.fold_in(seeds[8], 71), part)
    final_gain = jnp.clip(1.0 + 0.1 * jax.random.normal(seeds[7], (D,), jnp.float32), 0.5, 1.5).astype(jnp.bfloat16)
    return dict(points_in=points_in, hidden_weight=hidden_weight, output_weight=output_weight, point_owner=point_owner, point_node=point_node, point_weight=point_weight, proj_weight=proj_weight, final_gain=final_gain)


def rms_rows(values):
    return values * lax.rsqrt(lax.optimization_barrier(jnp.mean(values * values, axis=-1, keepdims=True)) + 1e-06)

def point_block(row_block, hidden_weight, output_weight):
    normed = rms_rows(row_block.astype(jnp.float32)).astype(jnp.bfloat16)
    hidden = jax.nn.gelu(jnp.dot(normed, hidden_weight, preferred_element_type=jnp.float32), approximate=False).astype(jnp.bfloat16)
    return (row_block.astype(jnp.float32) + jnp.dot(hidden, output_weight, preferred_element_type=jnp.float32)).astype(jnp.bfloat16)

def attend_block(query_block, key_rows, value_rows):
    scores = jnp.einsum('qhd,khd->hqk', query_block.astype(jnp.float32), key_rows.astype(jnp.float32)) * DH ** (-0.5)
    highest = lax.optimization_barrier(jnp.max(scores, axis=-1, keepdims=True))
    exps = jnp.exp(scores - highest)
    weights = exps.astype(jnp.bfloat16)
    summed = jnp.einsum('hqk,khd->qhd', weights.astype(jnp.float32), value_rows.astype(jnp.float32))
    return summed / jnp.transpose(lax.optimization_barrier(jnp.sum(exps, axis=-1)))[:, :, None]

def reference(points_in, hidden_weight, output_weight, point_owner, point_node, point_weight, proj_weight, final_gain):

    def one_block(row_block):
        return point_block(row_block, hidden_weight, output_weight)
    features = lax.map(one_block, points_in.reshape(N_BLK, P_DEV, D)).reshape(POINTS, D)
    node_index = (point_owner[:, 0] * S_DEV + point_node).astype(jnp.int32)
    weight_float = point_weight.astype(jnp.float32)
    weighted = weight_float[:, None] * features.astype(jnp.float32)
    pooled_sums = jax.ops.segment_sum(weighted, node_index, num_segments=NSUP)
    totals = jax.ops.segment_sum(weight_float, node_index, num_segments=NSUP)
    pooled = pooled_sums / (1.0 + totals[:, None])
    normed_nodes = rms_rows(pooled).astype(jnp.bfloat16)
    projected = jnp.dot(normed_nodes, proj_weight, preferred_element_type=jnp.float32).astype(jnp.bfloat16)
    block_rows = math.gcd(NSUP, 512)
    queries = projected[:, :D].reshape(NSUP // block_rows, block_rows, HEADS, DH)
    key_rows = projected[:, D:2 * D].reshape(NSUP, HEADS, DH)
    value_rows = projected[:, 2 * D:].reshape(NSUP, HEADS, DH)

    def attend(query_block):
        return attend_block(query_block, key_rows, value_rows)
    attended = lax.map(attend, queries).reshape(NSUP, D)
    return (rms_rows(attended) * final_gain.astype(jnp.float32)).astype(jnp.bfloat16)
```

```python
import functools

import jax
import jax.numpy as jnp
from jax import lax
from jax.experimental import pallas as pl
from jax.experimental.pallas import tpu as pltpu
from jax.sharding import PartitionSpec as P

HEADS = 12
S_DEV = 32
MESH = pl.DeviceIdType.MESH
F32, BF16 = jnp.float32, jnp.bfloat16


def rms_rows(values):
    return values * lax.rsqrt(jnp.mean(values * values, axis=-1, keepdims=True) + 1e-06)


def gelu(values):
    return values * (0.5 + 0.5 * lax.erf(values * 0.7071067811865476))


def kernel(
    n,
    owner_hbm,
    node_hbm,
    weight_hbm,
    gain_hbm,
    points_hbm,
    w1_hbm,
    w2_hbm,
    proj_hbm,
    out_ref,
    owner_ref,
    node_ref,
    weight_ref,
    gain_ref,
    points_ref,
    w1,
    w2,
    proj,
    normed,
    hidden,
    coeffs,
    feats,
    tot,
    tot_a,
    tot_b,
    tot_c,
    send_a,
    recv_a,
    keep_a,
    send_b,
    recv_b,
    keep_b,
    send_c,
    recv_c,
    keep_c,
    rows_g,
    keyval,
    small_sem,
    points_sem,
    w1_sem,
    w2_sem,
    proj_sem,
    tot_send,
    tot_recv,
    totc_send,
    totc_recv,
    a_send,
    a_recv,
    b_send,
    b_recv,
    c_send,
    c_recv,
    line_send,
    twin_send,
    mate_send,
    g_recv,
):
    me = lax.axis_index("blk")
    points, width = points_ref.shape
    parts = w1_sem.shape[0]
    part = w1.shape[1] // parts
    chunks = w2_sem.shape[0]
    wide = width // chunks
    pieces = send_a.shape[0]
    lane = send_a.shape[2]
    per = pieces // chunks
    m = n // 4
    bit0, bit1, quad = lax.rem(me, 2), lax.rem(me // 2, 2), me // 4
    mate = me + 1 - 2 * bit0
    twin = me + 2 - 4 * bit1
    base = me - quad * 4

    barrier = pltpu.get_barrier_semaphore()

    def greet(k, _):
        pl.semaphore_signal(
            barrier, inc=1, device_id={"blk": lax.rem(me + k, n)}, device_id_type=MESH
        )
        return 0


    w1_copies = [
        pltpu.make_async_copy(
            w1_hbm.at[:, pl.ds(i * part, part)], w1.at[:, pl.ds(i * part, part)], w1_sem.at[i]
        )
        for i in range(parts)
    ]
    w2_copies = [
        pltpu.make_async_copy(
            w2_hbm.at[:, pl.ds(i * wide, wide)], w2.at[:, pl.ds(i * wide, wide)], w2_sem.at[i]
        )
        for i in range(chunks)
    ]
    proj_copy = pltpu.make_async_copy(proj_hbm, proj, proj_sem)
    points_copy = pltpu.make_async_copy(points_hbm, points_ref, points_sem)
    small_copies = [
        pltpu.make_async_copy(source, dest, small_sem.at[i])
        for i, (source, dest) in enumerate(
            (
                (owner_hbm, owner_ref),
                (node_hbm, node_ref),
                (weight_hbm, weight_ref),
                (gain_hbm, gain_ref),
            )
        )
    ]
    queue = w1_copies + w2_copies + [proj_copy]
    points_copy.start()
    for copy in small_copies:
        copy.start()
    for copy in queue[:2]:
        copy.start()
    lax.fori_loop(1, n, greet, 0)
    for copy in small_copies:
        copy.wait()

    owner = owner_ref[...]
    rel0 = lax.rem(owner + bit0, 2)
    rel1 = lax.rem(owner // 2 + bit1, 2)
    place = ((rel0 * 2 + rel1) * m + owner // 4) * S_DEV + node_ref[...]
    weights = weight_ref[...].astype(F32)
    group = 128
    for start in range(0, n * S_DEV, group):
        ids = start + lax.broadcasted_iota(jnp.int32, (group, points), 0)
        coeffs[pl.ds(start, group), :] = jnp.where(ids == place, weights, 0.0).astype(BF16)
        tot[start // group] = lax.dot_general(
            jnp.ones((8, points), BF16),
            coeffs[pl.ds(start, group), :],
            (((1,), (1,)), ((), ())),
            preferred_element_type=F32,
        )

    points_copy.wait()
    queue[2].start()
    normed[...] = rms_rows(points_ref[...].astype(F32)).astype(BF16)

    for i in range(parts):
        w1_copies[i].wait()
        if i + 3 < len(queue):
            queue[i + 3].start()
        cols = pl.ds(i * part, part)
        up = jnp.dot(normed[...], w1[:, cols], preferred_element_type=F32)
        hidden[:, cols] = gelu(up).astype(BF16)

    for copy in queue[parts + 3 :]:
        copy.start()
    pl.semaphore_wait(barrier, n - 1)

    def loop(low, high, act):
        def run(k, _):
            act(k)
            return 0

        lax.fori_loop(low, high, run, 0)

    tiles = tot.shape[0]

    def tot_a_copy():
        return pltpu.make_async_remote_copy(
            src_ref=tot.at[pl.ds(tiles // 2, tiles // 2)],
            dst_ref=tot_a,
            send_sem=tot_send.at[0],
            recv_sem=tot_recv.at[0],
            device_id={"blk": mate},
            device_id_type=MESH,
        )

    def tot_b_copy():
        return pltpu.make_async_remote_copy(
            src_ref=tot_a.at[pl.ds(tiles // 4, tiles // 4)],
            dst_ref=tot_b,
            send_sem=tot_send.at[1],
            recv_sem=tot_recv.at[1],
            device_id={"blk": twin},
            device_id_type=MESH,
        )

    def tot_c_copy(k):
        dest = lax.rem(quad + k, m)
        return pltpu.make_async_remote_copy(
            src_ref=tot_b.at[dest * S_DEV // group],
            dst_ref=tot_c.at[k - 1],
            send_sem=totc_send.at[k - 1],
            recv_sem=totc_recv.at[k - 1],
            device_id={"blk": base + dest * 4},
            device_id_type=MESH,
        )

    def a_copy(c):
        return pltpu.make_async_remote_copy(
            src_ref=send_a.at[c],
            dst_ref=recv_a.at[c],
            send_sem=a_send.at[c],
            recv_sem=a_recv.at[c],
            device_id={"blk": mate},
            device_id_type=MESH,
        )

    def b_copy(c):
        return pltpu.make_async_remote_copy(
            src_ref=send_b.at[c],
            dst_ref=recv_b.at[c],
            send_sem=b_send.at[c],
            recv_sem=b_recv.at[c],
            device_id={"blk": twin},
            device_id_type=MESH,
        )

    def c_copy(c, k):
        dest = lax.rem(quad + k, m)
        return pltpu.make_async_remote_copy(
            src_ref=send_c.at[dest, c],
            dst_ref=recv_c.at[c, k - 1],
            send_sem=c_send.at[c, k - 1],
            recv_sem=c_recv.at[c, k - 1],
            device_id={"blk": base + dest * 4},
            device_id_type=MESH,
        )

    half, quarter = n // 2 * S_DEV, m * S_DEV

    def features_of(c):
        w2_copies[c].wait()
        cols = pl.ds(c * wide, wide)
        block = points // 4
        for r in range(4):
            rows = pl.ds(r * block, block)
            down = jnp.dot(hidden[rows, :], w2[:, cols], preferred_element_type=F32)
            feats[c, rows] = (points_ref[rows, cols].astype(F32) + down).astype(BF16)

    def stage_a(c):
        far = jnp.dot(coeffs[pl.ds(half, half), :], feats[c], preferred_element_type=F32)
        for j in range(per):
            send_a[c * per + j] = far[:, j * lane : (j + 1) * lane].astype(BF16)
            a_copy(c * per + j).start()
        near = jnp.dot(coeffs[pl.ds(0, half), :], feats[c], preferred_element_type=F32)
        for j in range(per):
            keep_a[c * per + j] = near[:, j * lane : (j + 1) * lane].astype(keep_a.dtype)

    def stage_b(p):
        a_copy(p).wait_recv()
        far = pl.ds(quarter, quarter)
        near = pl.ds(0, quarter)
        send_b[p] = (keep_a[p, far].astype(F32) + recv_a[p, far].astype(F32)).astype(BF16)
        b_copy(p).start()
        keep_b[p] = keep_a[p, near].astype(F32) + recv_a[p, near].astype(F32)

    def stage_c(p):
        b_copy(p).wait_recv()
        total = (keep_b[p] + recv_b[p].astype(F32)).reshape(m, S_DEV, lane)
        keep_c[p] = total
        for q in range(m):
            send_c[q, p] = total[q].astype(BF16)

        def send(k, _):
            c_copy(p, k).start()
            return 0

        lax.fori_loop(1, m, send, 0)

    def each(stage, c):
        if 0 <= c < chunks:
            for p in range(c * per, (c + 1) * per):
                stage(p)

    tot_a_copy().start()
    for c in range(chunks):
        features_of(c)
        if c == 1:
            tot_a_copy().wait()
            tot_a[...] = tot[pl.ds(0, tiles // 2)] + tot_a[...]
            tot_b_copy().start()
        each(stage_b, c - 1)
        stage_a(c)
    if chunks == 1:
        tot_a_copy().wait()
        tot_a[...] = tot[pl.ds(0, tiles // 2)] + tot_a[...]
        tot_b_copy().start()
    each(stage_b, chunks - 1)
    tot_b_copy().wait()
    tot_b[...] = tot_a[pl.ds(0, tiles // 4)] + tot_b[...]
    loop(1, m, lambda k: tot_c_copy(k).start())
    for c in range(chunks):
        each(stage_c, c)

    def take_total(k, total):
        tot_c_copy(k).wait()
        return total + tot_c[k - 1]

    totals_row = lax.fori_loop(1, m, take_total, tot_b[quad * S_DEV // group])[0:1, :]
    spot = lax.rem(quad * S_DEV, group)
    lanes = lax.broadcasted_iota(jnp.int32, (S_DEV, group), 1)
    rows = lax.broadcasted_iota(jnp.int32, (S_DEV, group), 0)
    totals = jnp.sum(jnp.where(lanes == rows + spot, totals_row, 0.0), axis=1, keepdims=True)

    sums = []
    for c in range(pieces):

        def take(k, total, c=c):
            c_copy(c, k).wait()
            return total + recv_c[c, k - 1].astype(F32)

        sums.append(lax.fori_loop(1, m, take, keep_c[c, quad]))
    pooled = jnp.concatenate(sums, axis=1) / (1.0 + totals)
    mine = rms_rows(pooled).astype(BF16)
    rows_g[0] = mine

    def g_copy(slot, to_slot, send_sem, dest):
        return pltpu.make_async_remote_copy(
            src_ref=rows_g.at[slot],
            dst_ref=rows_g.at[to_slot],
            send_sem=send_sem,
            recv_sem=g_recv.at[to_slot],
            device_id={"blk": dest},
            device_id_type=MESH,
        )

    def line_copy(k):
        return g_copy(0, k, line_send.at[k - 1], base + lax.rem(quad + k, m) * 4)

    def twin_copy(k):
        return g_copy(k, m + k, twin_send.at[k], twin)

    def mate_copy(k):
        return g_copy(k, 2 * m + k, mate_send.at[k], mate)

    def share(k):
        twin_copy(k).start()
        mate_copy(k).start()

    loop(1, m, lambda k: line_copy(k).start())
    share(0)

    proj_copy.wait()
    queries = jnp.dot(mine, proj[:, :width], preferred_element_type=F32).astype(BF16)
    queries = queries * jnp.asarray((width // HEADS) ** -0.5, BF16)

    def on_line(k):
        line_copy(k).wait_recv()
        share(k)

    loop(1, m, on_line)

    def project(low, count):
        block = rows_g[pl.ds(low, count)].reshape(count * S_DEV, width)
        keyval[pl.ds(low * S_DEV, count * S_DEV), :] = jnp.dot(
            block, proj[:, width:], preferred_element_type=F32
        ).astype(BF16)

    project(0, m)

    def take_twin(k):
        twin_copy(k).wait_recv()
        mate_copy(m + k).start()

    loop(0, m, take_twin)
    project(m, m)
    loop(0, m, lambda k: mate_copy(k).wait_recv())
    project(2 * m, m)
    loop(m, 2 * m, lambda k: mate_copy(k).wait_recv())
    project(3 * m, m)

    head = width // HEADS
    pack = 256 // head
    span = pack * head
    column_head = lax.broadcasted_iota(jnp.int32, (S_DEV, span), 1) // head
    outs = []
    for g in range(HEADS // pack):
        block = queries[:, g * span : (g + 1) * span]
        stacked = jnp.concatenate(
            [jnp.where(column_head == h, block, jnp.zeros_like(block)) for h in range(pack)], axis=0
        )
        scores = lax.dot_general(
            stacked,
            keyval[:, pl.ds(g * span, span)],
            (((1,), (1,)), ((), ())),
            preferred_element_type=F32,
        )
        exps = jnp.exp(scores - jnp.max(scores, axis=-1, keepdims=True))
        mixed = jnp.dot(
            exps.astype(BF16), keyval[:, pl.ds(width + g * span, span)], preferred_element_type=F32
        ) / jnp.sum(exps, axis=-1, keepdims=True)
        piece = mixed[:S_DEV]
        for h in range(1, pack):
            piece = jnp.where(column_head == h, mixed[h * S_DEV : (h + 1) * S_DEV], piece)
        outs.append(piece)
    attended = jnp.concatenate(outs, axis=1)
    out_ref[...] = (rms_rows(attended) * gain_ref[...].astype(F32)[None, :]).astype(BF16)

    for c in range(pieces):
        a_copy(c).wait_send()
        b_copy(c).wait_send()
    loop(1, m, lambda k: line_copy(k).wait_send())
    loop(0, m, lambda k: twin_copy(k).wait_send())
    loop(0, 2 * m, lambda k: mate_copy(k).wait_send())


def body(
    points_in,
    hidden_weight,
    output_weight,
    point_owner,
    point_node,
    point_weight,
    proj_weight,
    final_gain,
):
    n = lax.axis_size("blk")
    points, width = points_in.shape
    inner = hidden_weight.shape[1]
    m = n // 4
    chunks = 3 if width % (3 * 256) == 0 else 1
    parts = 5 if inner % (5 * 256) == 0 else 1
    nodes = n * S_DEV
    keep_type = F32 if nodes <= 1024 else BF16
    vmem = pl.BlockSpec(memory_space=pltpu.VMEM)
    hbm = pl.BlockSpec(memory_space=pl.ANY)
    dma = pltpu.SemaphoreType.DMA
    pieces = width // 128
    normed = pl.pallas_call(
        functools.partial(kernel, n),
        out_shape=jax.ShapeDtypeStruct((S_DEV, width), BF16),
        in_specs=[hbm] * 8,
        out_specs=vmem,
        scratch_shapes=[
            pltpu.VMEM((1, points), jnp.int32),
            pltpu.VMEM((1, points), jnp.int32),
            pltpu.VMEM((1, points), jnp.int32),
            pltpu.VMEM((width,), BF16),
            pltpu.VMEM((points, width), BF16),
            pltpu.VMEM(hidden_weight.shape, BF16),
            pltpu.VMEM(output_weight.shape, BF16),
            pltpu.VMEM(proj_weight.shape, BF16),
            pltpu.VMEM((points, width), BF16),
            pltpu.VMEM((points, inner), BF16),
            pltpu.VMEM((nodes, points), BF16),
            pltpu.VMEM((chunks, points, width // chunks), BF16),
            pltpu.VMEM((nodes // 128, 8, 128), F32),
            pltpu.VMEM((nodes // 256, 8, 128), F32),
            pltpu.VMEM((nodes // 512, 8, 128), F32),
            pltpu.VMEM((m - 1, 8, 128), F32),
            pltpu.VMEM((pieces, nodes // 2, 128), BF16),
            pltpu.VMEM((pieces, nodes // 2, 128), BF16),
            pltpu.VMEM((pieces, nodes // 2, 128), keep_type),
            pltpu.VMEM((pieces, nodes // 4, 128), BF16),
            pltpu.VMEM((pieces, nodes // 4, 128), BF16),
            pltpu.VMEM((pieces, nodes // 4, 128), F32),
            pltpu.VMEM((m, pieces, S_DEV, 128), BF16),
            pltpu.VMEM((pieces, m - 1, S_DEV, 128), BF16),
            pltpu.VMEM((pieces, m, S_DEV, 128), F32),
            pltpu.VMEM((n, S_DEV, width), BF16),
            pltpu.VMEM((nodes, 2 * width), BF16),
            dma((4,)),
            dma,
            dma((parts,)),
            dma((chunks,)),
            dma,
            dma((2,)),
            dma((2,)),
            dma((m - 1,)),
            dma((m - 1,)),
            dma((pieces,)),
            dma((pieces,)),
            dma((pieces,)),
            dma((pieces,)),
            dma((pieces, m - 1)),
            dma((pieces, m - 1)),
            dma((m - 1,)),
            dma((m,)),
            dma((2 * m,)),
            dma((n,)),
        ],
        compiler_params=pltpu.CompilerParams(
            collective_id=0, has_side_effects=True, vmem_limit_bytes=66_000_000
        ),
    )(
        point_owner.reshape(1, points),
        point_node.reshape(1, points),
        point_weight.reshape(1, points),
        final_gain,
        points_in,
        hidden_weight,
        output_weight,
        proj_weight,
    )
    return normed


def solution(mesh):
    placed = (
        P(("groups", "blk"), None),
        P(),
        P(),
        P(("groups", "blk"), None),
        P(("groups", "blk")),
        P(("groups", "blk")),
        P(),
        P(),
    )
    return jax.shard_map(
        body, mesh=mesh, in_specs=placed, out_specs=P(("groups", "blk"), None), check_vma=False
    )
```

```python
import functools

import jax
import jax.numpy as jnp
from jax import lax
from jax.experimental import pallas as pl
from jax.experimental.pallas import tpu as pltpu
from jax.sharding import PartitionSpec as P

HEADS = 12
S_DEV = 32
MESH = pl.DeviceIdType.MESH
F32, BF16 = jnp.float32, jnp.bfloat16


def rms_rows(values):
    return values * lax.rsqrt(jnp.mean(values * values, axis=-1, keepdims=True) + 1e-06)


def gelu(values):
    return values * (0.5 + 0.5 * lax.erf(values * 0.7071067811865476))


def kernel(
    n,
    owner_hbm,
    node_hbm,
    weight_hbm,
    gain_hbm,
    points_hbm,
    w1_hbm,
    w2_hbm,
    proj_hbm,
    out_ref,
    owner_ref,
    node_ref,
    weight_ref,
    gain_ref,
    points_ref,
    w1,
    w2,
    proj,
    normed,
    hidden,
    coeffs,
    feats,
    tot,
    tot_a,
    tot_b,
    tot_c,
    send_a,
    recv_a,
    keep_a,
    send_b,
    recv_b,
    keep_b,
    send_c,
    recv_c,
    keep_c,
    rows_g,
    keyval,
    small_sem,
    points_sem,
    w1_sem,
    w2_sem,
    proj_sem,
    tot_send,
    tot_recv,
    totc_send,
    totc_recv,
    a_send,
    a_recv,
    b_send,
    b_recv,
    c_send,
    c_recv,
    line_send,
    line_recv,
    twin_send,
    twin_recv,
    mate_send,
    mate_recv,
):
    me = lax.axis_index("blk")
    points, width = points_ref.shape
    parts = w1_sem.shape[0]
    part = w1.shape[1] // parts
    chunks = w2_sem.shape[0]
    wide = width // chunks
    pieces = send_a.shape[0]
    lane = send_a.shape[2]
    per = pieces // chunks
    m = n // 4
    bit0, bit1, quad = lax.rem(me, 2), lax.rem(me // 2, 2), me // 4
    mate = me + 1 - 2 * bit0
    twin = me + 2 - 4 * bit1
    base = me - quad * 4

    barrier = pltpu.get_barrier_semaphore()

    def greet(k, _):
        pl.semaphore_signal(
            barrier, inc=1, device_id={"blk": lax.rem(me + k, n)}, device_id_type=MESH
        )
        return 0


    w1_copies = [
        pltpu.make_async_copy(
            w1_hbm.at[:, pl.ds(i * part, part)], w1.at[:, pl.ds(i * part, part)], w1_sem.at[i]
        )
        for i in range(parts)
    ]
    w2_copies = [
        pltpu.make_async_copy(
            w2_hbm.at[:, pl.ds(i * wide, wide)], w2.at[:, pl.ds(i * wide, wide)], w2_sem.at[i]
        )
        for i in range(chunks)
    ]
    proj_copy = pltpu.make_async_copy(proj_hbm, proj, proj_sem)
    points_copy = pltpu.make_async_copy(points_hbm, points_ref, points_sem)
    small_copies = [
        pltpu.make_async_copy(source, dest, small_sem.at[i])
        for i, (source, dest) in enumerate(
            (
                (owner_hbm, owner_ref),
                (node_hbm, node_ref),
                (weight_hbm, weight_ref),
                (gain_hbm, gain_ref),
            )
        )
    ]
    queue = w1_copies + w2_copies + [proj_copy]
    points_copy.start()
    for copy in small_copies:
        copy.start()
    for copy in queue[:2]:
        copy.start()
    lax.fori_loop(1, n, greet, 0)
    for copy in small_copies:
        copy.wait()

    owner = owner_ref[...]
    rel0 = lax.rem(owner + bit0, 2)
    rel1 = lax.rem(owner // 2 + bit1, 2)
    place = ((rel0 * 2 + rel1) * m + owner // 4) * S_DEV + node_ref[...]
    weights = weight_ref[...].astype(F32)
    group = 128
    for start in range(0, n * S_DEV, group):
        ids = start + lax.broadcasted_iota(jnp.int32, (group, points), 0)
        coeffs[pl.ds(start, group), :] = jnp.where(ids == place, weights, 0.0).astype(BF16)
        tot[start // group] = lax.dot_general(
            jnp.ones((8, points), BF16),
            coeffs[pl.ds(start, group), :],
            (((1,), (1,)), ((), ())),
            preferred_element_type=F32,
        )

    points_copy.wait()
    queue[2].start()
    normed[...] = rms_rows(points_ref[...].astype(F32)).astype(BF16)

    for i in range(parts):
        w1_copies[i].wait()
        if i + 3 < len(queue):
            queue[i + 3].start()
        cols = pl.ds(i * part, part)
        up = jnp.dot(normed[...], w1[:, cols], preferred_element_type=F32)
        hidden[:, cols] = gelu(up).astype(BF16)

    for copy in queue[parts + 3 :]:
        copy.start()
    pl.semaphore_wait(barrier, n - 1)

    def loop(low, high, act):
        if high - low <= 4:
            for k in range(low, high):
                act(k)
            return

        def run(k, _):
            act(k)
            return 0

        lax.fori_loop(low, high, run, 0)

    def gather(low, high, act, total):
        if high - low <= 4:
            for k in range(low, high):
                total = act(k, total)
            return total
        return lax.fori_loop(low, high, act, total)

    def peer(k):
        if m != 4:
            return lax.rem(quad + k, m)
        return (quad + 1 - 2 * lax.rem(quad, 2), quad + 2 - 4 * (quad // 2), 3 - quad)[k - 1]

    tiles = tot.shape[0]

    def tot_a_copy():
        return pltpu.make_async_remote_copy(
            src_ref=tot.at[pl.ds(tiles // 2, tiles // 2)],
            dst_ref=tot_a,
            send_sem=tot_send.at[0],
            recv_sem=tot_recv.at[0],
            device_id={"blk": mate},
            device_id_type=MESH,
        )

    def tot_b_copy():
        return pltpu.make_async_remote_copy(
            src_ref=tot_a.at[pl.ds(tiles // 4, tiles // 4)],
            dst_ref=tot_b,
            send_sem=tot_send.at[1],
            recv_sem=tot_recv.at[1],
            device_id={"blk": twin},
            device_id_type=MESH,
        )

    def tot_c_copy(k):
        dest = peer(k)
        return pltpu.make_async_remote_copy(
            src_ref=tot_b.at[dest * S_DEV // group],
            dst_ref=tot_c.at[k - 1],
            send_sem=totc_send.at[k - 1],
            recv_sem=totc_recv.at[k - 1],
            device_id={"blk": base + dest * 4},
            device_id_type=MESH,
        )

    def a_copy(c):
        return pltpu.make_async_remote_copy(
            src_ref=send_a.at[c],
            dst_ref=recv_a.at[c],
            send_sem=a_send.at[c],
            recv_sem=a_recv.at[c],
            device_id={"blk": mate},
            device_id_type=MESH,
        )

    def b_copy(c):
        return pltpu.make_async_remote_copy(
            src_ref=send_b.at[c],
            dst_ref=recv_b.at[c],
            send_sem=b_send.at[c],
            recv_sem=b_recv.at[c],
            device_id={"blk": twin},
            device_id_type=MESH,
        )

    def c_copy(c, k):
        dest = peer(k)
        return pltpu.make_async_remote_copy(
            src_ref=send_c.at[dest, c],
            dst_ref=recv_c.at[c, k - 1],
            send_sem=c_send.at[c, k - 1],
            recv_sem=c_recv.at[c, k - 1],
            device_id={"blk": base + dest * 4},
            device_id_type=MESH,
        )

    half, quarter = n // 2 * S_DEV, m * S_DEV

    def features_of(c):
        w2_copies[c].wait()
        cols = pl.ds(c * wide, wide)
        block = points // 4
        for r in range(4):
            rows = pl.ds(r * block, block)
            down = jnp.dot(hidden[rows, :], w2[:, cols], preferred_element_type=F32)
            feats[c, rows] = (points_ref[rows, cols].astype(F32) + down).astype(BF16)

    def stage_a(c):
        far = jnp.dot(coeffs[pl.ds(half, half), :], feats[c], preferred_element_type=F32)
        for j in range(per):
            send_a[c * per + j] = far[:, j * lane : (j + 1) * lane].astype(BF16)
            a_copy(c * per + j).start()
        near = jnp.dot(coeffs[pl.ds(0, half), :], feats[c], preferred_element_type=F32)
        for j in range(per):
            keep_a[c * per + j] = near[:, j * lane : (j + 1) * lane].astype(keep_a.dtype)

    def stage_b(p):
        a_copy(p).wait_recv()
        far = pl.ds(quarter, quarter)
        near = pl.ds(0, quarter)
        send_b[p] = (keep_a[p, far].astype(F32) + recv_a[p, far].astype(F32)).astype(BF16)
        b_copy(p).start()
        keep_b[p] = keep_a[p, near].astype(F32) + recv_a[p, near].astype(F32)

    def stage_c(p):
        b_copy(p).wait_recv()
        total = (keep_b[p] + recv_b[p].astype(F32)).reshape(m, S_DEV, lane)
        keep_c[p] = total
        for q in range(m):
            send_c[q, p] = total[q].astype(BF16)

        loop(1, m, lambda k: c_copy(p, m - k).start())

    def each(stage, c):
        if 0 <= c < chunks:
            for p in range(c * per, (c + 1) * per):
                stage(p)

    tot_a_copy().start()
    for c in range(chunks):
        features_of(c)
        if c == 1:
            tot_a_copy().wait()
            tot_a[...] = tot[pl.ds(0, tiles // 2)] + tot_a[...]
            tot_b_copy().start()
        each(stage_b, c - 1)
        stage_a(c)
    if chunks == 1:
        tot_a_copy().wait()
        tot_a[...] = tot[pl.ds(0, tiles // 2)] + tot_a[...]
        tot_b_copy().start()
    each(stage_b, chunks - 1)
    tot_b_copy().wait()
    tot_b[...] = tot_a[pl.ds(0, tiles // 4)] + tot_b[...]
    loop(1, m, lambda k: tot_c_copy(k).start())
    for c in range(chunks):
        each(stage_c, c)

    def take_total(k, total):
        tot_c_copy(k).wait()
        return total + tot_c[k - 1]

    totals_row = gather(1, m, take_total, tot_b[quad * S_DEV // group])[0:1, :]
    spot = lax.rem(quad * S_DEV, group)
    lanes = lax.broadcasted_iota(jnp.int32, (S_DEV, group), 1)
    rows = lax.broadcasted_iota(jnp.int32, (S_DEV, group), 0)
    totals = jnp.sum(jnp.where(lanes == rows + spot, totals_row, 0.0), axis=1, keepdims=True)

    def g_copy(slot, to_slot, count, c, send_sem, recv_sem, dest):
        cols = pl.ds(c * wide, wide)
        return pltpu.make_async_remote_copy(
            src_ref=rows_g.at[pl.ds(slot, count), :, cols],
            dst_ref=rows_g.at[pl.ds(to_slot, count), :, cols],
            send_sem=send_sem,
            recv_sem=recv_sem,
            device_id={"blk": dest},
            device_id_type=MESH,
        )

    def line_copy(c, k):
        return g_copy(
            0, k, 1, c, line_send.at[c, k - 1], line_recv.at[c, k - 1], base + peer(k) * 4
        )

    def twin_copy(c, k):
        return g_copy(k, m + k, 1, c, twin_send.at[c, k], twin_recv.at[c, k], twin)

    def mate_copy(c, h):
        return g_copy(h * m, (2 + h) * m, m, c, mate_send.at[c, h], mate_recv.at[c, h], mate)

    for c in range(chunks):
        sums = []
        for p in range(c * per, (c + 1) * per):

            def take(k, total, p=p):
                c_copy(p, k).wait()
                return total + recv_c[p, k - 1].astype(F32)

            sums.append(gather(1, m, take, keep_c[p, quad]))
        pooled = jnp.concatenate(sums, axis=1) / (1.0 + totals)
        rows_g[0, :, c * wide : (c + 1) * wide] = pooled.astype(BF16)
        loop(1, m, lambda k, c=c: line_copy(c, m - k).start())
        twin_copy(c, 0).start()

    def on_line(c, k):
        line_copy(c, k).wait_recv()
        twin_copy(c, k).start()

    for c in range(chunks):
        loop(1, m, lambda k, c=c: on_line(c, k))
        mate_copy(c, 0).start()

    def normed_rows(low, count):
        block = rows_g[pl.ds(low, count)].reshape(count * S_DEV, width)
        wider = block.astype(F32)
        return block, lax.rsqrt(jnp.mean(wider * wider, axis=-1, keepdims=True) + 1e-06)

    proj_copy.wait()
    mine, scale = normed_rows(0, 1)
    queries = (jnp.dot(mine, proj[:, :width], preferred_element_type=F32) * scale).astype(BF16)
    queries = queries * jnp.asarray((width // HEADS) ** -0.5, BF16)

    def project(low, count):
        block, scale = normed_rows(low, count)
        keyval[pl.ds(low * S_DEV, count * S_DEV), :] = (
            jnp.dot(block, proj[:, width:], preferred_element_type=F32) * scale
        ).astype(BF16)

    def take_twin(c):
        loop(0, m, lambda k: twin_copy(c, k).wait_recv())
        mate_copy(c, 1).start()

    project(0, m)
    for c in range(chunks - 1):
        take_twin(c)
    for c in range(chunks):
        mate_copy(c, 0).wait_recv()
    project(2 * m, m)
    take_twin(chunks - 1)
    project(m, m)
    for c in range(chunks):
        mate_copy(c, 1).wait_recv()
    project(3 * m, m)

    head = width // HEADS
    pack = 256 // head
    span = pack * head
    column_head = lax.broadcasted_iota(jnp.int32, (S_DEV, span), 1) // head
    outs = []
    for g in range(HEADS // pack):
        block = queries[:, g * span : (g + 1) * span]
        stacked = jnp.concatenate(
            [jnp.where(column_head == h, block, jnp.zeros_like(block)) for h in range(pack)], axis=0
        )
        scores = lax.dot_general(
            stacked,
            keyval[:, pl.ds(g * span, span)],
            (((1,), (1,)), ((), ())),
            preferred_element_type=F32,
        )
        exps = jnp.exp(scores - jnp.max(scores, axis=-1, keepdims=True))
        mixed = jnp.dot(
            exps.astype(BF16), keyval[:, pl.ds(width + g * span, span)], preferred_element_type=F32
        ) / jnp.sum(exps, axis=-1, keepdims=True)
        piece = mixed[:S_DEV]
        for h in range(1, pack):
            piece = jnp.where(column_head == h, mixed[h * S_DEV : (h + 1) * S_DEV], piece)
        outs.append(piece)
    attended = jnp.concatenate(outs, axis=1)
    out_ref[...] = (rms_rows(attended) * gain_ref[...].astype(F32)[None, :]).astype(BF16)

    for c in range(pieces):
        a_copy(c).wait_send()
        b_copy(c).wait_send()
    for c in range(chunks):
        loop(1, m, lambda k, c=c: line_copy(c, k).wait_send())
        loop(0, m, lambda k, c=c: twin_copy(c, k).wait_send())
        mate_copy(c, 0).wait_send()
        mate_copy(c, 1).wait_send()


def body(
    points_in,
    hidden_weight,
    output_weight,
    point_owner,
    point_node,
    point_weight,
    proj_weight,
    final_gain,
):
    n = lax.axis_size("blk")
    points, width = points_in.shape
    inner = hidden_weight.shape[1]
    m = n // 4
    chunks = 3 if width % (3 * 256) == 0 else 1
    parts = 5 if inner % (5 * 256) == 0 else 1
    nodes = n * S_DEV
    keep_type = F32 if nodes <= 1024 else BF16
    vmem = pl.BlockSpec(memory_space=pltpu.VMEM)
    hbm = pl.BlockSpec(memory_space=pl.ANY)
    dma = pltpu.SemaphoreType.DMA
    pieces = width // 128
    normed = pl.pallas_call(
        functools.partial(kernel, n),
        out_shape=jax.ShapeDtypeStruct((S_DEV, width), BF16),
        in_specs=[hbm] * 8,
        out_specs=vmem,
        scratch_shapes=[
            pltpu.VMEM((1, points), jnp.int32),
            pltpu.VMEM((1, points), jnp.int32),
            pltpu.VMEM((1, points), jnp.int32),
            pltpu.VMEM((width,), BF16),
            pltpu.VMEM((points, width), BF16),
            pltpu.VMEM(hidden_weight.shape, BF16),
            pltpu.VMEM(output_weight.shape, BF16),
            pltpu.VMEM(proj_weight.shape, BF16),
            pltpu.VMEM((points, width), BF16),
            pltpu.VMEM((points, inner), BF16),
            pltpu.VMEM((nodes, points), BF16),
            pltpu.VMEM((chunks, points, width // chunks), BF16),
            pltpu.VMEM((nodes // 128, 8, 128), F32),
            pltpu.VMEM((nodes // 256, 8, 128), F32),
            pltpu.VMEM((nodes // 512, 8, 128), F32),
            pltpu.VMEM((m - 1, 8, 128), F32),
            pltpu.VMEM((pieces, nodes // 2, 128), BF16),
            pltpu.VMEM((pieces, nodes // 2, 128), BF16),
            pltpu.VMEM((pieces, nodes // 2, 128), keep_type),
            pltpu.VMEM((pieces, nodes // 4, 128), BF16),
            pltpu.VMEM((pieces, nodes // 4, 128), BF16),
            pltpu.VMEM((pieces, nodes // 4, 128), F32),
            pltpu.VMEM((m, pieces, S_DEV, 128), BF16),
            pltpu.VMEM((pieces, m - 1, S_DEV, 128), BF16),
            pltpu.VMEM((pieces, m, S_DEV, 128), F32),
            pltpu.VMEM((n, S_DEV, width), BF16),
            pltpu.VMEM((nodes, 2 * width), BF16),
            dma((4,)),
            dma,
            dma((parts,)),
            dma((chunks,)),
            dma,
            dma((2,)),
            dma((2,)),
            dma((m - 1,)),
            dma((m - 1,)),
            dma((pieces,)),
            dma((pieces,)),
            dma((pieces,)),
            dma((pieces,)),
            dma((pieces, m - 1)),
            dma((pieces, m - 1)),
            dma((chunks, m - 1)),
            dma((chunks, m - 1)),
            dma((chunks, m)),
            dma((chunks, m)),
            dma((chunks, 2)),
            dma((chunks, 2)),
        ],
        compiler_params=pltpu.CompilerParams(
            collective_id=0, has_side_effects=True, vmem_limit_bytes=66_000_000
        ),
    )(
        point_owner.reshape(1, points),
        point_node.reshape(1, points),
        point_weight.reshape(1, points),
        final_gain,
        points_in,
        hidden_weight,
        output_weight,
        proj_weight,
    )
    return normed


def solution(mesh):
    placed = (
        P(("groups", "blk"), None),
        P(),
        P(),
        P(("groups", "blk"), None),
        P(("groups", "blk")),
        P(("groups", "blk")),
        P(),
        P(),
    )
    return jax.shard_map(
        body, mesh=mesh, in_specs=placed, out_specs=P(("groups", "blk"), None), check_vma=False
    )
```

```python
import functools

import jax
import jax.numpy as jnp
from jax import lax
from jax.experimental import pallas as pl
from jax.experimental.pallas import tpu as pltpu
from jax.sharding import PartitionSpec as P

HEADS = 12
S_DEV = 32
MESH = pl.DeviceIdType.MESH
F32, BF16 = jnp.float32, jnp.bfloat16


def rms_rows(values):
    return values * lax.rsqrt(jnp.mean(values * values, axis=-1, keepdims=True) + 1e-06)


def gelu(values):
    return values * (0.5 + 0.5 * lax.erf(values * 0.7071067811865476))


def kernel(
    n,
    owner_hbm,
    node_hbm,
    weight_hbm,
    gain_hbm,
    points_hbm,
    w1_hbm,
    w2_hbm,
    proj_hbm,
    out_ref,
    owner_ref,
    node_ref,
    weight_ref,
    gain_ref,
    points_ref,
    w1,
    w2,
    proj,
    normed,
    hidden,
    coeffs,
    feats,
    tot,
    tot_a,
    tot_b,
    tot_c,
    send_a,
    recv_a,
    keep_a,
    send_b,
    recv_b,
    keep_b,
    send_c,
    recv_c,
    keep_c,
    rows_g,
    keyval,
    small_sem,
    points_sem,
    w1_sem,
    w2_sem,
    proj_sem,
    tot_send,
    tot_recv,
    totc_send,
    totc_recv,
    a_send,
    a_recv,
    b_send,
    b_recv,
    c_send,
    c_recv,
    line_send,
    line_recv,
    twin_send,
    twin_recv,
    mate_send,
    mate_recv,
):
    me = lax.axis_index("blk")
    points, width = points_ref.shape
    parts = w1_sem.shape[0]
    part = w1.shape[1] // parts
    chunks = w2_sem.shape[0]
    wide = width // chunks
    pieces = send_a.shape[0]
    lane = send_a.shape[2]
    per = pieces // chunks
    m = n // 4
    bit0, bit1, quad = lax.rem(me, 2), lax.rem(me // 2, 2), me // 4
    mate = me + 1 - 2 * bit0
    twin = me + 2 - 4 * bit1
    base = me - quad * 4

    barrier = pltpu.get_barrier_semaphore()

    def greet(k, _):
        pl.semaphore_signal(
            barrier, inc=1, device_id={"blk": lax.rem(me + k, n)}, device_id_type=MESH
        )
        return 0


    w1_copies = [
        pltpu.make_async_copy(
            w1_hbm.at[:, pl.ds(i * part, part)], w1.at[:, pl.ds(i * part, part)], w1_sem.at[i]
        )
        for i in range(parts)
    ]
    w2_copies = [
        pltpu.make_async_copy(
            w2_hbm.at[:, pl.ds(i * wide, wide)], w2.at[:, pl.ds(i * wide, wide)], w2_sem.at[i]
        )
        for i in range(chunks)
    ]
    proj_copy = pltpu.make_async_copy(proj_hbm, proj, proj_sem)
    points_copy = pltpu.make_async_copy(points_hbm, points_ref, points_sem)
    small_copies = [
        pltpu.make_async_copy(source, dest, small_sem.at[i])
        for i, (source, dest) in enumerate(
            (
                (owner_hbm, owner_ref),
                (node_hbm, node_ref),
                (weight_hbm, weight_ref),
                (gain_hbm, gain_ref),
            )
        )
    ]
    queue = w1_copies + w2_copies + [proj_copy]
    points_copy.start()
    for copy in small_copies:
        copy.start()
    for copy in queue[:2]:
        copy.start()
    lax.fori_loop(1, n, greet, 0)
    for copy in small_copies:
        copy.wait()

    owner = owner_ref[...]
    rel0 = lax.rem(owner + bit0, 2)
    rel1 = lax.rem(owner // 2 + bit1, 2)
    place = ((rel0 * 2 + rel1) * m + owner // 4) * S_DEV + node_ref[...]
    weights = weight_ref[...].astype(F32)
    group = 128
    for start in range(0, n * S_DEV, group):
        ids = start + lax.broadcasted_iota(jnp.int32, (group, points), 0)
        coeffs[pl.ds(start, group), :] = jnp.where(ids == place, weights, 0.0).astype(BF16)
        tot[start // group] = lax.dot_general(
            jnp.ones((8, points), BF16),
            coeffs[pl.ds(start, group), :],
            (((1,), (1,)), ((), ())),
            preferred_element_type=F32,
        )

    points_copy.wait()
    queue[2].start()
    normed[...] = rms_rows(points_ref[...].astype(F32)).astype(BF16)

    for i in range(parts):
        w1_copies[i].wait()
        if i + 3 < len(queue):
            queue[i + 3].start()
        cols = pl.ds(i * part, part)
        up = jnp.dot(normed[...], w1[:, cols], preferred_element_type=F32)
        hidden[:, cols] = gelu(up).astype(BF16)

    for copy in queue[parts + 3 :]:
        copy.start()
    pl.semaphore_wait(barrier, n - 1)

    def loop(low, high, act):
        if high - low <= 4:
            for k in range(low, high):
                act(k)
            return

        def run(k, _):
            act(k)
            return 0

        lax.fori_loop(low, high, run, 0)

    def gather(low, high, act, total):
        if high - low <= 4:
            for k in range(low, high):
                total = act(k, total)
            return total
        return lax.fori_loop(low, high, act, total)

    def peer(k):
        if m != 4:
            return lax.rem(quad + k, m)
        return (quad + 1 - 2 * lax.rem(quad, 2), quad + 2 - 4 * (quad // 2), 3 - quad)[k - 1]

    tiles = tot.shape[0]

    def tot_a_copy():
        return pltpu.make_async_remote_copy(
            src_ref=tot.at[pl.ds(tiles // 2, tiles // 2)],
            dst_ref=tot_a,
            send_sem=tot_send.at[0],
            recv_sem=tot_recv.at[0],
            device_id={"blk": mate},
            device_id_type=MESH,
        )

    def tot_b_copy():
        return pltpu.make_async_remote_copy(
            src_ref=tot_a.at[pl.ds(tiles // 4, tiles // 4)],
            dst_ref=tot_b,
            send_sem=tot_send.at[1],
            recv_sem=tot_recv.at[1],
            device_id={"blk": twin},
            device_id_type=MESH,
        )

    def tot_c_copy(k):
        dest = peer(k)
        return pltpu.make_async_remote_copy(
            src_ref=tot_b.at[dest * S_DEV // group],
            dst_ref=tot_c.at[k - 1],
            send_sem=totc_send.at[k - 1],
            recv_sem=totc_recv.at[k - 1],
            device_id={"blk": base + dest * 4},
            device_id_type=MESH,
        )

    def a_copy(c):
        return pltpu.make_async_remote_copy(
            src_ref=send_a.at[c],
            dst_ref=recv_a.at[c],
            send_sem=a_send.at[c],
            recv_sem=a_recv.at[c],
            device_id={"blk": mate},
            device_id_type=MESH,
        )

    def b_copy(c):
        return pltpu.make_async_remote_copy(
            src_ref=send_b.at[c],
            dst_ref=recv_b.at[c],
            send_sem=b_send.at[c],
            recv_sem=b_recv.at[c],
            device_id={"blk": twin},
            device_id_type=MESH,
        )

    def c_copy(c, k):
        dest = peer(k)
        return pltpu.make_async_remote_copy(
            src_ref=send_c.at[dest, c],
            dst_ref=recv_c.at[c, k - 1],
            send_sem=c_send.at[c, k - 1],
            recv_sem=c_recv.at[c, k - 1],
            device_id={"blk": base + dest * 4},
            device_id_type=MESH,
        )

    half, quarter = n // 2 * S_DEV, m * S_DEV

    def features_of(c):
        w2_copies[c].wait()
        cols = pl.ds(c * wide, wide)
        block = points // 4
        for r in range(4):
            rows = pl.ds(r * block, block)
            down = jnp.dot(hidden[rows, :], w2[:, cols], preferred_element_type=F32)
            feats[c, rows] = (points_ref[rows, cols].astype(F32) + down).astype(BF16)

    def stage_a(c):
        far = jnp.dot(coeffs[pl.ds(half, half), :], feats[c], preferred_element_type=F32)
        for j in range(per):
            send_a[c * per + j] = far[:, j * lane : (j + 1) * lane].astype(BF16)
            a_copy(c * per + j).start()
        near = jnp.dot(coeffs[pl.ds(0, half), :], feats[c], preferred_element_type=F32)
        for j in range(per):
            keep_a[c * per + j] = near[:, j * lane : (j + 1) * lane].astype(keep_a.dtype)

    def stage_b(p):
        a_copy(p).wait_recv()
        far = pl.ds(quarter, quarter)
        near = pl.ds(0, quarter)
        send_b[p] = (keep_a[p, far].astype(F32) + recv_a[p, far].astype(F32)).astype(BF16)
        b_copy(p).start()
        keep_b[p] = keep_a[p, near].astype(F32) + recv_a[p, near].astype(F32)

    def stage_c(p):
        b_copy(p).wait_recv()
        total = (keep_b[p] + recv_b[p].astype(F32)).reshape(m, S_DEV, lane)
        keep_c[p] = total
        for q in range(m):
            send_c[q, p] = total[q].astype(BF16)

        loop(1, m, lambda k: c_copy(p, m - k).start())

    def each(stage, c):
        if 0 <= c < chunks:
            for p in range(c * per, (c + 1) * per):
                stage(p)

    tot_a_copy().start()
    for c in range(chunks):
        features_of(c)
        if c == 1:
            tot_a_copy().wait()
            tot_a[...] = tot[pl.ds(0, tiles // 2)] + tot_a[...]
            tot_b_copy().start()
        each(stage_b, c - 1)
        stage_a(c)
    if chunks == 1:
        tot_a_copy().wait()
        tot_a[...] = tot[pl.ds(0, tiles // 2)] + tot_a[...]
        tot_b_copy().start()
    each(stage_b, chunks - 1)
    tot_b_copy().wait()
    tot_b[...] = tot_a[pl.ds(0, tiles // 4)] + tot_b[...]
    loop(1, m, lambda k: tot_c_copy(k).start())
    for c in range(chunks):
        each(stage_c, c)

    def take_total(k, total):
        tot_c_copy(k).wait()
        return total + tot_c[k - 1]

    totals_row = gather(1, m, take_total, tot_b[quad * S_DEV // group])[0:1, :]
    spot = lax.rem(quad * S_DEV, group)
    lanes = lax.broadcasted_iota(jnp.int32, (S_DEV, group), 1)
    rows = lax.broadcasted_iota(jnp.int32, (S_DEV, group), 0)
    totals = jnp.sum(jnp.where(lanes == rows + spot, totals_row, 0.0), axis=1, keepdims=True)

    def g_copy(slot, to_slot, count, c, send_sem, recv_sem, dest):
        cols = pl.ds(c * wide, wide)
        return pltpu.make_async_remote_copy(
            src_ref=rows_g.at[pl.ds(slot, count), :, cols],
            dst_ref=rows_g.at[pl.ds(to_slot, count), :, cols],
            send_sem=send_sem,
            recv_sem=recv_sem,
            device_id={"blk": dest},
            device_id_type=MESH,
        )

    def line_copy(c, k):
        return g_copy(
            0, k, 1, c, line_send.at[c, k - 1], line_recv.at[c, k - 1], base + peer(k) * 4
        )

    def twin_copy(c, k):
        return g_copy(k, m + k, 1, c, twin_send.at[c, k], twin_recv.at[c, k], twin)

    def mate_copy(c, h):
        return g_copy(h * m, (2 + h) * m, m, c, mate_send.at[c, h], mate_recv.at[c, h], mate)

    for c in range(chunks):
        sums = []
        for p in range(c * per, (c + 1) * per):

            def take(k, total, p=p):
                c_copy(p, k).wait()
                return total + recv_c[p, k - 1].astype(F32)

            sums.append(gather(1, m, take, keep_c[p, quad]))
        pooled = jnp.concatenate(sums, axis=1) / (1.0 + totals)
        rows_g[0, :, c * wide : (c + 1) * wide] = pooled.astype(BF16)
        loop(1, m, lambda k, c=c: line_copy(c, m - k).start())
        twin_copy(c, 0).start()

    def on_line(c, k):
        line_copy(c, k).wait_recv()
        twin_copy(c, k).start()

    for c in range(chunks):
        loop(1, m, lambda k, c=c: on_line(c, k))
        mate_copy(c, 0).start()

    def normed_rows(low, count):
        block = rows_g[pl.ds(low, count)].reshape(count * S_DEV, width)
        wider = block.astype(F32)
        return block, lax.rsqrt(jnp.mean(wider * wider, axis=-1, keepdims=True) + 1e-06)

    proj_copy.wait()
    mine, scale = normed_rows(0, 1)
    queries = (jnp.dot(mine, proj[:, :width], preferred_element_type=F32) * scale).astype(BF16)
    queries = queries * jnp.asarray((width // HEADS) ** -0.5, BF16)

    def project(low, count):
        block, scale = normed_rows(low, count)
        keyval[pl.ds(low * S_DEV, count * S_DEV), :] = (
            jnp.dot(block, proj[:, width:], preferred_element_type=F32) * scale
        ).astype(BF16)

    def take_twin(c):
        loop(0, m, lambda k: twin_copy(c, k).wait_recv())
        mate_copy(c, 1).start()

    project(0, m)
    for c in range(chunks - 1):
        take_twin(c)
    for c in range(chunks):
        mate_copy(c, 0).wait_recv()
    project(2 * m, m)
    take_twin(chunks - 1)
    project(m, m)
    for c in range(chunks):
        mate_copy(c, 1).wait_recv()
    project(3 * m, m)

    head = width // HEADS
    pack = 256 // head
    span = pack * head
    column_head = lax.broadcasted_iota(jnp.int32, (S_DEV, span), 1) // head
    outs = []
    for g in range(HEADS // pack):
        block = queries[:, g * span : (g + 1) * span]
        stacked = jnp.concatenate(
            [jnp.where(column_head == h, block, jnp.zeros_like(block)) for h in range(pack)], axis=0
        )
        scores = lax.dot_general(
            stacked,
            keyval[:, pl.ds(g * span, span)],
            (((1,), (1,)), ((), ())),
            preferred_element_type=F32,
        )
        exps = jnp.exp(scores - jnp.max(scores, axis=-1, keepdims=True))
        mixed = jnp.dot(
            exps.astype(BF16), keyval[:, pl.ds(width + g * span, span)], preferred_element_type=F32
        ) / jnp.sum(exps, axis=-1, keepdims=True)
        piece = mixed[:S_DEV]
        for h in range(1, pack):
            piece = jnp.where(column_head == h, mixed[h * S_DEV : (h + 1) * S_DEV], piece)
        outs.append(piece)
    attended = jnp.concatenate(outs, axis=1)
    out_ref[...] = (rms_rows(attended) * gain_ref[...].astype(F32)[None, :]).astype(BF16)

    for c in range(pieces):
        a_copy(c).wait_send()
        b_copy(c).wait_send()
    for c in range(chunks):
        loop(1, m, lambda k, c=c: line_copy(c, k).wait_send())
        loop(0, m, lambda k, c=c: twin_copy(c, k).wait_send())
        mate_copy(c, 0).wait_send()
        mate_copy(c, 1).wait_send()


def body(
    points_in,
    hidden_weight,
    output_weight,
    point_owner,
    point_node,
    point_weight,
    proj_weight,
    final_gain,
):
    n = lax.axis_size("blk")
    points, width = points_in.shape
    inner = hidden_weight.shape[1]
    m = n // 4
    chunks = 3 if width % (3 * 256) == 0 else 1
    parts = 5 if inner % (5 * 256) == 0 else 1
    nodes = n * S_DEV
    keep_type = F32 if nodes <= 1024 else BF16
    vmem = pl.BlockSpec(memory_space=pltpu.VMEM)
    hbm = pl.BlockSpec(memory_space=pl.ANY)
    dma = pltpu.SemaphoreType.DMA
    pieces = width // 128
    normed = pl.pallas_call(
        functools.partial(kernel, n),
        out_shape=jax.ShapeDtypeStruct((S_DEV, width), BF16),
        in_specs=[hbm] * 8,
        out_specs=vmem,
        scratch_shapes=[
            pltpu.VMEM((1, points), jnp.int32),
            pltpu.VMEM((1, points), jnp.int32),
            pltpu.VMEM((1, points), jnp.int32),
            pltpu.VMEM((width,), BF16),
            pltpu.VMEM((points, width), BF16),
            pltpu.VMEM(hidden_weight.shape, BF16),
            pltpu.VMEM(output_weight.shape, BF16),
            pltpu.VMEM(proj_weight.shape, BF16),
            pltpu.VMEM((points, width), BF16),
            pltpu.VMEM((points, inner), BF16),
            pltpu.VMEM((nodes, points), BF16),
            pltpu.VMEM((chunks, points, width // chunks), BF16),
            pltpu.VMEM((nodes // 128, 8, 128), F32),
            pltpu.VMEM((nodes // 256, 8, 128), F32),
            pltpu.VMEM((nodes // 512, 8, 128), F32),
            pltpu.VMEM((m - 1, 8, 128), F32),
            pltpu.VMEM((pieces, nodes // 2, 128), BF16),
            pltpu.VMEM((pieces, nodes // 2, 128), BF16),
            pltpu.VMEM((pieces, nodes // 2, 128), keep_type),
            pltpu.VMEM((pieces, nodes // 4, 128), BF16),
            pltpu.VMEM((pieces, nodes // 4, 128), BF16),
            pltpu.VMEM((pieces, nodes // 4, 128), F32),
            pltpu.VMEM((m, pieces, S_DEV, 128), BF16),
            pltpu.VMEM((pieces, m - 1, S_DEV, 128), BF16),
            pltpu.VMEM((pieces, m, S_DEV, 128), F32),
            pltpu.VMEM((n, S_DEV, width), BF16),
            pltpu.VMEM((nodes, 2 * width), BF16),
            dma((4,)),
            dma,
            dma((parts,)),
            dma((chunks,)),
            dma,
            dma((2,)),
            dma((2,)),
            dma((m - 1,)),
            dma((m - 1,)),
            dma((pieces,)),
            dma((pieces,)),
            dma((pieces,)),
            dma((pieces,)),
            dma((pieces, m - 1)),
            dma((pieces, m - 1)),
            dma((chunks, m - 1)),
            dma((chunks, m - 1)),
            dma((chunks, m)),
            dma((chunks, m)),
            dma((chunks, 2)),
            dma((chunks, 2)),
        ],
        compiler_params=pltpu.CompilerParams(
            collective_id=0, has_side_effects=True, vmem_limit_bytes=40_000_000 if nodes <= 1024 else 66_000_000
        ),
    )(
        *(
            pltpu.with_memory_space_constraint(x, pltpu.HBM)
            for x in (
                point_owner.reshape(1, points),
                point_node.reshape(1, points),
                point_weight.reshape(1, points),
                final_gain,
                points_in,
                hidden_weight,
                output_weight,
                proj_weight,
            )
        )
    )
    return normed


def solution(mesh):
    placed = (
        P(("groups", "blk"), None),
        P(),
        P(),
        P(("groups", "blk"), None),
        P(("groups", "blk")),
        P(("groups", "blk")),
        P(),
        P(),
    )
    return jax.shard_map(
        body, mesh=mesh, in_specs=placed, out_specs=P(("groups", "blk"), None), check_vma=False
    )
```

```python
import functools

import jax
import jax.numpy as jnp
from jax import lax
from jax.experimental import pallas as pl
from jax.experimental.pallas import tpu as pltpu
from jax.sharding import PartitionSpec as P

HEADS = 12
S_DEV = 32
MESH = pl.DeviceIdType.MESH
F32, BF16 = jnp.float32, jnp.bfloat16


def rms_rows(values):
    return values * lax.rsqrt(jnp.mean(values * values, axis=-1, keepdims=True) + 1e-06)


def gelu(values):
    return values * (0.5 + 0.5 * lax.erf(values * 0.7071067811865476))


def kernel(
    n,
    owner_hbm,
    node_hbm,
    weight_hbm,
    gain_hbm,
    points_hbm,
    w1_hbm,
    w2_hbm,
    proj_hbm,
    out_ref,
    owner_ref,
    node_ref,
    weight_ref,
    gain_ref,
    points_ref,
    w1,
    w2,
    proj,
    normed,
    hidden,
    coeffs,
    feats,
    tot,
    tot_a,
    tot_b,
    tot_c,
    send_a,
    recv_a,
    keep_a,
    send_b,
    recv_b,
    keep_b,
    send_c,
    recv_c,
    keep_c,
    rows_g,
    keyval,
    small_sem,
    points_sem,
    w1_sem,
    w2_sem,
    proj_sem,
    tot_send,
    tot_recv,
    totc_send,
    totc_recv,
    a_send,
    a_recv,
    b_send,
    b_recv,
    c_send,
    c_recv,
    line_send,
    line_recv,
    twin_send,
    twin_recv,
    mate_send,
    mate_recv,
):
    me = lax.axis_index("blk")
    points, width = points_ref.shape
    parts = w1_sem.shape[0]
    part = w1.shape[1] // parts
    chunks = w2_sem.shape[0]
    wide = width // chunks
    pieces = send_a.shape[0]
    lane = send_a.shape[2]
    per = pieces // chunks
    m = n // 4
    bit0, bit1, quad = lax.rem(me, 2), lax.rem(me // 2, 2), me // 4
    mate = me + 1 - 2 * bit0
    twin = me + 2 - 4 * bit1
    base = me - quad * 4

    barrier = pltpu.get_barrier_semaphore()

    def greet(k, _):
        pl.semaphore_signal(
            barrier, inc=1, device_id={"blk": lax.rem(me + k, n)}, device_id_type=MESH
        )
        return 0


    w1_copies = [
        pltpu.make_async_copy(
            w1_hbm.at[:, pl.ds(i * part, part)], w1.at[:, pl.ds(i * part, part)], w1_sem.at[i]
        )
        for i in range(parts)
    ]
    w2_copies = [
        pltpu.make_async_copy(
            w2_hbm.at[:, pl.ds(i * wide, wide)], w2.at[:, pl.ds(i * wide, wide)], w2_sem.at[i]
        )
        for i in range(chunks)
    ]
    proj_copy = pltpu.make_async_copy(proj_hbm, proj, proj_sem)
    points_copy = pltpu.make_async_copy(points_hbm, points_ref, points_sem)
    small_copies = [
        pltpu.make_async_copy(source, dest, small_sem.at[i])
        for i, (source, dest) in enumerate(
            (
                (owner_hbm, owner_ref),
                (node_hbm, node_ref),
                (weight_hbm, weight_ref),
                (gain_hbm, gain_ref),
            )
        )
    ]
    points_copy.start()
    for copy in small_copies:
        copy.start()
    for copy in w1_copies[:3]:
        copy.start()
    lax.fori_loop(1, n, greet, 0)
    for copy in small_copies:
        copy.wait()

    owner = owner_ref[...]
    rel0 = lax.rem(owner + bit0, 2)
    rel1 = lax.rem(owner // 2 + bit1, 2)
    place = ((rel0 * 2 + rel1) * m + owner // 4) * S_DEV + node_ref[...]
    weights = weight_ref[...].astype(F32)
    group = 128
    for start in range(0, n * S_DEV, group):
        ids = start + lax.broadcasted_iota(jnp.int32, (group, points), 0)
        coeffs[pl.ds(start, group), :] = jnp.where(ids == place, weights, 0.0).astype(BF16)
        tot[start // group] = lax.dot_general(
            jnp.ones((8, points), BF16),
            coeffs[pl.ds(start, group), :],
            (((1,), (1,)), ((), ())),
            preferred_element_type=F32,
        )

    points_copy.wait()
    for copy in w1_copies[3:]:
        copy.start()
    normed[...] = rms_rows(points_ref[...].astype(F32)).astype(BF16)

    for i in range(parts):
        if i == 0:
            for copy in w1_copies[:2]:
                copy.wait()
            for copy in w2_copies:
                copy.start()
        if i == 2:
            for copy in w1_copies[2:]:
                copy.wait()
        cols = pl.ds(i * part, part)
        up = jnp.dot(normed[...], w1[:, cols], preferred_element_type=F32)
        hidden[:, cols] = gelu(up).astype(BF16)

    proj_copy.start()
    pl.semaphore_wait(barrier, n - 1)

    def loop(low, high, act):
        if high - low <= 4:
            for k in range(low, high):
                act(k)
            return

        def run(k, _):
            act(k)
            return 0

        lax.fori_loop(low, high, run, 0)

    def gather(low, high, act, total):
        if high - low <= 4:
            for k in range(low, high):
                total = act(k, total)
            return total
        return lax.fori_loop(low, high, act, total)

    def peer(k):
        if m != 4:
            return lax.rem(quad + k, m)
        return (quad + 1 - 2 * lax.rem(quad, 2), quad + 2 - 4 * (quad // 2), 3 - quad)[k - 1]

    tiles = tot.shape[0]

    def tot_a_copy():
        return pltpu.make_async_remote_copy(
            src_ref=tot.at[pl.ds(tiles // 2, tiles // 2)],
            dst_ref=tot_a,
            send_sem=tot_send.at[0],
            recv_sem=tot_recv.at[0],
            device_id={"blk": mate},
            device_id_type=MESH,
        )

    def tot_b_copy():
        return pltpu.make_async_remote_copy(
            src_ref=tot_a.at[pl.ds(tiles // 4, tiles // 4)],
            dst_ref=tot_b,
            send_sem=tot_send.at[1],
            recv_sem=tot_recv.at[1],
            device_id={"blk": twin},
            device_id_type=MESH,
        )

    def tot_c_copy(k):
        dest = peer(k)
        return pltpu.make_async_remote_copy(
            src_ref=tot_b.at[dest * S_DEV // group],
            dst_ref=tot_c.at[k - 1],
            send_sem=totc_send.at[k - 1],
            recv_sem=totc_recv.at[k - 1],
            device_id={"blk": base + dest * 4},
            device_id_type=MESH,
        )

    def a_copy(c):
        return pltpu.make_async_remote_copy(
            src_ref=send_a.at[c],
            dst_ref=recv_a.at[c],
            send_sem=a_send.at[c],
            recv_sem=a_recv.at[c],
            device_id={"blk": mate},
            device_id_type=MESH,
        )

    def b_copy(c):
        return pltpu.make_async_remote_copy(
            src_ref=send_b.at[c],
            dst_ref=recv_b.at[c],
            send_sem=b_send.at[c],
            recv_sem=b_recv.at[c],
            device_id={"blk": twin},
            device_id_type=MESH,
        )

    def c_copy(c, k):
        dest = peer(k)
        return pltpu.make_async_remote_copy(
            src_ref=send_c.at[dest, c],
            dst_ref=recv_c.at[c, k - 1],
            send_sem=c_send.at[c, k - 1],
            recv_sem=c_recv.at[c, k - 1],
            device_id={"blk": base + dest * 4},
            device_id_type=MESH,
        )

    half, quarter = n // 2 * S_DEV, m * S_DEV

    def features_of(c):
        if c == 0:
            for copy in w2_copies:
                copy.wait()
        cols = pl.ds(c * wide, wide)
        block = points // 4
        for r in range(4):
            rows = pl.ds(r * block, block)
            down = jnp.dot(hidden[rows, :], w2[:, cols], preferred_element_type=F32)
            feats[c, rows] = (points_ref[rows, cols].astype(F32) + down).astype(BF16)

    def stage_a(c):
        far = jnp.dot(coeffs[pl.ds(half, half), :], feats[c], preferred_element_type=F32)
        for j in range(per):
            send_a[c * per + j] = far[:, j * lane : (j + 1) * lane].astype(BF16)
            a_copy(c * per + j).start()
        near = jnp.dot(coeffs[pl.ds(0, half), :], feats[c], preferred_element_type=F32)
        for j in range(per):
            keep_a[c * per + j] = near[:, j * lane : (j + 1) * lane].astype(keep_a.dtype)

    def stage_b(p):
        a_copy(p).wait_recv()
        far = pl.ds(quarter, quarter)
        near = pl.ds(0, quarter)
        send_b[p] = (keep_a[p, far].astype(F32) + recv_a[p, far].astype(F32)).astype(BF16)
        b_copy(p).start()
        keep_b[p] = keep_a[p, near].astype(F32) + recv_a[p, near].astype(F32)

    def stage_c(p):
        b_copy(p).wait_recv()
        total = (keep_b[p] + recv_b[p].astype(F32)).reshape(m, S_DEV, lane)
        keep_c[p] = total
        for q in range(m):
            send_c[q, p] = total[q].astype(BF16)

        loop(1, m, lambda k: c_copy(p, k).start())

    def each(stage, c):
        if 0 <= c < chunks:
            for p in range(c * per, (c + 1) * per):
                stage(p)

    tot_a_copy().start()
    for c in range(chunks):
        features_of(c)
        if c == 1:
            tot_a_copy().wait()
            tot_a[...] = tot[pl.ds(0, tiles // 2)] + tot_a[...]
            tot_b_copy().start()
        each(stage_b, c - 1)
        stage_a(c)
    if chunks == 1:
        tot_a_copy().wait()
        tot_a[...] = tot[pl.ds(0, tiles // 2)] + tot_a[...]
        tot_b_copy().start()
    each(stage_b, chunks - 1)
    tot_b_copy().wait()
    tot_b[...] = tot_a[pl.ds(0, tiles // 4)] + tot_b[...]
    loop(1, m, lambda k: tot_c_copy(k).start())
    for c in range(chunks):
        each(stage_c, c)

    def take_total(k, total):
        tot_c_copy(k).wait()
        return total + tot_c[k - 1]

    totals_row = gather(1, m, take_total, tot_b[quad * S_DEV // group])[0:1, :]
    spot = lax.rem(quad * S_DEV, group)
    lanes = lax.broadcasted_iota(jnp.int32, (S_DEV, group), 1)
    rows = lax.broadcasted_iota(jnp.int32, (S_DEV, group), 0)
    totals = jnp.sum(jnp.where(lanes == rows + spot, totals_row, 0.0), axis=1, keepdims=True)

    def g_copy(slot, to_slot, count, c, send_sem, recv_sem, dest):
        cols = pl.ds(c * wide, wide)
        return pltpu.make_async_remote_copy(
            src_ref=rows_g.at[pl.ds(slot, count), :, cols],
            dst_ref=rows_g.at[pl.ds(to_slot, count), :, cols],
            send_sem=send_sem,
            recv_sem=recv_sem,
            device_id={"blk": dest},
            device_id_type=MESH,
        )

    def line_copy(c, k):
        return g_copy(
            0, k, 1, c, line_send.at[c, k - 1], line_recv.at[c, k - 1], base + peer(k) * 4
        )

    def twin_copy(c, k):
        return g_copy(k, m + k, 1, c, twin_send.at[c, k], twin_recv.at[c, k], twin)

    def mate_copy(c, h):
        return g_copy(h * m, (2 + h) * m, m, c, mate_send.at[c, h], mate_recv.at[c, h], mate)

    for c in range(chunks):
        sums = []
        for p in range(c * per, (c + 1) * per):

            def take(k, total, p=p):
                c_copy(p, k).wait()
                return total + recv_c[p, k - 1].astype(F32)

            sums.append(gather(1, m, take, keep_c[p, quad]))
        pooled = jnp.concatenate(sums, axis=1) / (1.0 + totals)
        rows_g[0, :, c * wide : (c + 1) * wide] = pooled.astype(BF16)
        loop(1, m, lambda k, c=c: line_copy(c, k).start())
        twin_copy(c, 0).start()

    def on_line(c, k):
        line_copy(c, k).wait_recv()
        twin_copy(c, k).start()

    for c in range(chunks):
        loop(1, m, lambda k, c=c: on_line(c, k))
        mate_copy(c, 0).start()

    def normed_rows(low, count):
        block = rows_g[pl.ds(low, count)].reshape(count * S_DEV, width)
        wider = block.astype(F32)
        return block, lax.rsqrt(jnp.mean(wider * wider, axis=-1, keepdims=True) + 1e-06)

    proj_copy.wait()
    mine, scale = normed_rows(0, 1)
    queries = (jnp.dot(mine, proj[:, :width], preferred_element_type=F32) * scale).astype(BF16)
    queries = queries * jnp.asarray((width // HEADS) ** -0.5, BF16)

    def project(low, count):
        block, scale = normed_rows(low, count)
        keyval[pl.ds(low * S_DEV, count * S_DEV), :] = (
            jnp.dot(block, proj[:, width:], preferred_element_type=F32) * scale
        ).astype(BF16)

    def take_twin(c):
        loop(0, m, lambda k: twin_copy(c, k).wait_recv())
        mate_copy(c, 1).start()

    project(0, m)
    for c in range(chunks - 1):
        take_twin(c)
    for c in range(chunks):
        mate_copy(c, 0).wait_recv()
    project(2 * m, m)
    take_twin(chunks - 1)
    project(m, m)
    for c in range(chunks):
        mate_copy(c, 1).wait_recv()
    project(3 * m, m)

    head = width // HEADS
    pack = 256 // head
    span = pack * head
    column_head = lax.broadcasted_iota(jnp.int32, (S_DEV, span), 1) // head
    outs = []
    for g in range(HEADS // pack):
        block = queries[:, g * span : (g + 1) * span]
        stacked = jnp.concatenate(
            [jnp.where(column_head == h, block, jnp.zeros_like(block)) for h in range(pack)], axis=0
        )
        scores = lax.dot_general(
            stacked,
            keyval[:, pl.ds(g * span, span)],
            (((1,), (1,)), ((), ())),
            preferred_element_type=F32,
        )
        exps = jnp.exp(scores - jnp.max(scores, axis=-1, keepdims=True))
        mixed = jnp.dot(
            exps.astype(BF16), keyval[:, pl.ds(width + g * span, span)], preferred_element_type=F32
        ) / jnp.sum(exps, axis=-1, keepdims=True)
        piece = mixed[:S_DEV]
        for h in range(1, pack):
            piece = jnp.where(column_head == h, mixed[h * S_DEV : (h + 1) * S_DEV], piece)
        outs.append(piece)
    attended = jnp.concatenate(outs, axis=1)
    out_ref[...] = (rms_rows(attended) * gain_ref[...].astype(F32)[None, :]).astype(BF16)

    for c in range(pieces):
        a_copy(c).wait_send()
        b_copy(c).wait_send()
    for c in range(chunks):
        loop(1, m, lambda k, c=c: line_copy(c, k).wait_send())
        loop(0, m, lambda k, c=c: twin_copy(c, k).wait_send())
        mate_copy(c, 0).wait_send()
        mate_copy(c, 1).wait_send()


def body(
    points_in,
    hidden_weight,
    output_weight,
    point_owner,
    point_node,
    point_weight,
    proj_weight,
    final_gain,
):
    n = lax.axis_size("blk")
    points, width = points_in.shape
    inner = hidden_weight.shape[1]
    m = n // 4
    chunks = 3 if width % (3 * 256) == 0 else 1
    parts = 5 if inner % (5 * 256) == 0 else 1
    nodes = n * S_DEV
    keep_type = F32 if nodes <= 1024 else BF16
    vmem = pl.BlockSpec(memory_space=pltpu.VMEM)
    hbm = pl.BlockSpec(memory_space=pl.ANY)
    dma = pltpu.SemaphoreType.DMA
    pieces = width // 128
    normed = pl.pallas_call(
        functools.partial(kernel, n),
        out_shape=jax.ShapeDtypeStruct((S_DEV, width), BF16),
        in_specs=[hbm] * 8,
        out_specs=vmem,
        scratch_shapes=[
            pltpu.VMEM((1, points), jnp.int32),
            pltpu.VMEM((1, points), jnp.int32),
            pltpu.VMEM((1, points), jnp.int32),
            pltpu.VMEM((width,), BF16),
            pltpu.VMEM((points, width), BF16),
            pltpu.VMEM(hidden_weight.shape, BF16),
            pltpu.VMEM(output_weight.shape, BF16),
            pltpu.VMEM(proj_weight.shape, BF16),
            pltpu.VMEM((points, width), BF16),
            pltpu.VMEM((points, inner), BF16),
            pltpu.VMEM((nodes, points), BF16),
            pltpu.VMEM((chunks, points, width // chunks), BF16),
            pltpu.VMEM((nodes // 128, 8, 128), F32),
            pltpu.VMEM((nodes // 256, 8, 128), F32),
            pltpu.VMEM((nodes // 512, 8, 128), F32),
            pltpu.VMEM((m - 1, 8, 128), F32),
            pltpu.VMEM((pieces, nodes // 2, 128), BF16),
            pltpu.VMEM((pieces, nodes // 2, 128), BF16),
            pltpu.VMEM((pieces, nodes // 2, 128), keep_type),
            pltpu.VMEM((pieces, nodes // 4, 128), BF16),
            pltpu.VMEM((pieces, nodes // 4, 128), BF16),
            pltpu.VMEM((pieces, nodes // 4, 128), F32),
            pltpu.VMEM((m, pieces, S_DEV, 128), BF16),
            pltpu.VMEM((pieces, m - 1, S_DEV, 128), BF16),
            pltpu.VMEM((pieces, m, S_DEV, 128), F32),
            pltpu.VMEM((n, S_DEV, width), BF16),
            pltpu.VMEM((nodes, 2 * width), BF16),
            dma((4,)),
            dma,
            dma((parts,)),
            dma((chunks,)),
            dma,
            dma((2,)),
            dma((2,)),
            dma((m - 1,)),
            dma((m - 1,)),
            dma((pieces,)),
            dma((pieces,)),
            dma((pieces,)),
            dma((pieces,)),
            dma((pieces, m - 1)),
            dma((pieces, m - 1)),
            dma((chunks, m - 1)),
            dma((chunks, m - 1)),
            dma((chunks, m)),
            dma((chunks, m)),
            dma((chunks, 2)),
            dma((chunks, 2)),
        ],
        compiler_params=pltpu.CompilerParams(
            collective_id=0, has_side_effects=True, vmem_limit_bytes=40_000_000 if nodes <= 1024 else 66_000_000
        ),
    )(
        *(
            pltpu.with_memory_space_constraint(x, pltpu.HBM)
            for x in (
                point_owner.reshape(1, points),
                point_node.reshape(1, points),
                point_weight.reshape(1, points),
                final_gain,
                points_in,
                hidden_weight,
                output_weight,
                proj_weight,
            )
        )
    )
    return normed


def solution(mesh):
    placed = (
        P(("groups", "blk"), None),
        P(),
        P(),
        P(("groups", "blk"), None),
        P(("groups", "blk")),
        P(("groups", "blk")),
        P(),
        P(),
    )
    return jax.shard_map(
        body, mesh=mesh, in_specs=placed, out_specs=P(("groups", "blk"), None), check_vma=False
    )
```

```python
import functools

import jax
import jax.numpy as jnp
from jax import lax
from jax.experimental import pallas as pl
from jax.experimental.pallas import tpu as pltpu
from jax.sharding import PartitionSpec as P

HEADS = 12
S_DEV = 32
MESH = pl.DeviceIdType.MESH
F32, BF16 = jnp.float32, jnp.bfloat16


def rms_rows(values):
    return values * lax.rsqrt(jnp.mean(values * values, axis=-1, keepdims=True) + 1e-06)


def gelu(values):
    return values * (0.5 + 0.5 * lax.erf(values * 0.7071067811865476))


def kernel(
    n,
    owner_hbm,
    node_hbm,
    weight_hbm,
    gain_hbm,
    points_hbm,
    w1_hbm,
    w2_hbm,
    proj_hbm,
    out_ref,
    owner_ref,
    node_ref,
    weight_ref,
    gain_ref,
    points_ref,
    w1,
    w2,
    proj,
    normed,
    hidden,
    coeffs,
    feats,
    tot,
    tot_a,
    tot_b,
    tot_c,
    send_a,
    recv_a,
    keep_a,
    send_b,
    recv_b,
    keep_b,
    send_c,
    recv_c,
    keep_c,
    rows_g,
    keyval,
    lastly,
    small_sem,
    points_sem,
    w1_sem,
    w2_sem,
    proj_sem,
    tot_send,
    tot_recv,
    totc_send,
    totc_recv,
    a_send,
    a_recv,
    b_send,
    b_recv,
    c_send,
    c_recv,
    line_send,
    line_recv,
    twin_send,
    twin_recv,
    mate_send,
    mate_recv,
    single_send,
    single_recv,
):
    me = lax.axis_index("blk")
    points, width = points_ref.shape
    parts = w1_sem.shape[0]
    part = w1.shape[1] // parts
    chunks = w2_sem.shape[0]
    wide = width // chunks
    pieces = send_a.shape[0]
    lane = send_a.shape[2]
    per = pieces // chunks
    m = n // 4
    bit0, bit1, quad = lax.rem(me, 2), lax.rem(me // 2, 2), me // 4
    mate = me + 1 - 2 * bit0
    twin = me + 2 - 4 * bit1
    base = me - quad * 4

    barrier = pltpu.get_barrier_semaphore()

    def greet(k, _):
        pl.semaphore_signal(
            barrier, inc=1, device_id={"blk": lax.rem(me + k, n)}, device_id_type=MESH
        )
        return 0


    w1_copies = [
        pltpu.make_async_copy(
            w1_hbm.at[:, pl.ds(i * part, part)], w1.at[:, pl.ds(i * part, part)], w1_sem.at[i]
        )
        for i in range(parts)
    ]
    w2_copies = [
        pltpu.make_async_copy(
            w2_hbm.at[:, pl.ds(i * wide, wide)], w2.at[:, pl.ds(i * wide, wide)], w2_sem.at[i]
        )
        for i in range(chunks)
    ]
    proj_copy = pltpu.make_async_copy(proj_hbm, proj, proj_sem)
    points_copy = pltpu.make_async_copy(points_hbm, points_ref, points_sem)
    small_copies = [
        pltpu.make_async_copy(source, dest, small_sem.at[i])
        for i, (source, dest) in enumerate(
            (
                (owner_hbm, owner_ref),
                (node_hbm, node_ref),
                (weight_hbm, weight_ref),
                (gain_hbm, gain_ref),
            )
        )
    ]
    points_copy.start()
    for copy in small_copies:
        copy.start()
    for copy in w1_copies[:3]:
        copy.start()
    lax.fori_loop(1, n, greet, 0)
    for copy in small_copies:
        copy.wait()

    owner = owner_ref[...]
    rel0 = lax.rem(owner + bit0, 2)
    rel1 = lax.rem(owner // 2 + bit1, 2)
    place = ((rel0 * 2 + rel1) * m + owner // 4) * S_DEV + node_ref[...]
    weights = weight_ref[...].astype(F32)
    group = 128
    for start in range(0, n * S_DEV, group):
        ids = start + lax.broadcasted_iota(jnp.int32, (group, points), 0)
        coeffs[pl.ds(start, group), :] = jnp.where(ids == place, weights, 0.0).astype(BF16)
        tot[start // group] = lax.dot_general(
            jnp.ones((8, points), BF16),
            coeffs[pl.ds(start, group), :],
            (((1,), (1,)), ((), ())),
            preferred_element_type=F32,
        )

    points_copy.wait()
    for copy in w1_copies[3:]:
        copy.start()
    normed[...] = rms_rows(points_ref[...].astype(F32)).astype(BF16)

    for i in range(parts):
        if i == 0:
            for copy in w1_copies[:2]:
                copy.wait()
            for copy in w2_copies:
                copy.start()
        if i == 2:
            for copy in w1_copies[2:]:
                copy.wait()
        cols = pl.ds(i * part, part)
        up = jnp.dot(normed[...], w1[:, cols], preferred_element_type=F32)
        hidden[:, cols] = gelu(up).astype(BF16)

    proj_copy.start()
    pl.semaphore_wait(barrier, n - 1)

    def loop(low, high, act):
        if high - low <= 4:
            for k in range(low, high):
                act(k)
            return

        def run(k, _):
            act(k)
            return 0

        lax.fori_loop(low, high, run, 0)

    def gather(low, high, act, total):
        if high - low <= 4:
            for k in range(low, high):
                total = act(k, total)
            return total
        return lax.fori_loop(low, high, act, total)

    def peer(k):
        if m != 4:
            return lax.rem(quad + k, m)
        return (quad + 1 - 2 * lax.rem(quad, 2), quad + 2 - 4 * (quad // 2), 3 - quad)[k - 1]

    tiles = tot.shape[0]

    def tot_a_copy():
        return pltpu.make_async_remote_copy(
            src_ref=tot.at[pl.ds(tiles // 2, tiles // 2)],
            dst_ref=tot_a,
            send_sem=tot_send.at[0],
            recv_sem=tot_recv.at[0],
            device_id={"blk": mate},
            device_id_type=MESH,
        )

    def tot_b_copy():
        return pltpu.make_async_remote_copy(
            src_ref=tot_a.at[pl.ds(tiles // 4, tiles // 4)],
            dst_ref=tot_b,
            send_sem=tot_send.at[1],
            recv_sem=tot_recv.at[1],
            device_id={"blk": twin},
            device_id_type=MESH,
        )

    def tot_c_copy(k):
        dest = peer(k)
        return pltpu.make_async_remote_copy(
            src_ref=tot_b.at[dest * S_DEV // group],
            dst_ref=tot_c.at[k - 1],
            send_sem=totc_send.at[k - 1],
            recv_sem=totc_recv.at[k - 1],
            device_id={"blk": base + dest * 4},
            device_id_type=MESH,
        )

    def a_copy(c):
        return pltpu.make_async_remote_copy(
            src_ref=send_a.at[c],
            dst_ref=recv_a.at[c],
            send_sem=a_send.at[c],
            recv_sem=a_recv.at[c],
            device_id={"blk": mate},
            device_id_type=MESH,
        )

    def b_copy(c):
        return pltpu.make_async_remote_copy(
            src_ref=send_b.at[c],
            dst_ref=recv_b.at[c],
            send_sem=b_send.at[c],
            recv_sem=b_recv.at[c],
            device_id={"blk": twin},
            device_id_type=MESH,
        )

    def c_copy(c, k):
        dest = peer(k)
        return pltpu.make_async_remote_copy(
            src_ref=send_c.at[dest, c],
            dst_ref=recv_c.at[c, k - 1],
            send_sem=c_send.at[c, k - 1],
            recv_sem=c_recv.at[c, k - 1],
            device_id={"blk": base + dest * 4},
            device_id_type=MESH,
        )

    half, quarter = n // 2 * S_DEV, m * S_DEV

    def features_of(c):
        if c == 0:
            for copy in w2_copies:
                copy.wait()
        cols = pl.ds(c * wide, wide)
        block = points // 4
        for r in range(4):
            rows = pl.ds(r * block, block)
            down = jnp.dot(hidden[rows, :], w2[:, cols], preferred_element_type=F32)
            feats[c, rows] = (points_ref[rows, cols].astype(F32) + down).astype(BF16)

    def stage_a(c):
        far = jnp.dot(coeffs[pl.ds(half, half), :], feats[c], preferred_element_type=F32)
        for j in range(per):
            send_a[c * per + j] = far[:, j * lane : (j + 1) * lane].astype(BF16)
            a_copy(c * per + j).start()
        near = jnp.dot(coeffs[pl.ds(0, half), :], feats[c], preferred_element_type=F32)
        for j in range(per):
            keep_a[c * per + j] = near[:, j * lane : (j + 1) * lane].astype(keep_a.dtype)

    def stage_b(p):
        a_copy(p).wait_recv()
        far = pl.ds(quarter, quarter)
        near = pl.ds(0, quarter)
        send_b[p] = (keep_a[p, far].astype(F32) + recv_a[p, far].astype(F32)).astype(BF16)
        b_copy(p).start()
        keep_b[p] = keep_a[p, near].astype(F32) + recv_a[p, near].astype(F32)

    def stage_c(p):
        b_copy(p).wait_recv()
        total = (keep_b[p] + recv_b[p].astype(F32)).reshape(m, S_DEV, lane)
        keep_c[p] = total
        for q in range(m):
            send_c[q, p] = total[q].astype(BF16)

        loop(1, m, lambda k: c_copy(p, k).start())

    def each(stage, c):
        if 0 <= c < chunks:
            for p in range(c * per, (c + 1) * per):
                stage(p)

    tot_a_copy().start()
    for c in range(chunks):
        features_of(c)
        if c == 1:
            tot_a_copy().wait()
            tot_a[...] = tot[pl.ds(0, tiles // 2)] + tot_a[...]
            tot_b_copy().start()
        each(stage_b, c - 1)
        stage_a(c)
    if chunks == 1:
        tot_a_copy().wait()
        tot_a[...] = tot[pl.ds(0, tiles // 2)] + tot_a[...]
        tot_b_copy().start()
    each(stage_b, chunks - 1)
    tot_b_copy().wait()
    tot_b[...] = tot_a[pl.ds(0, tiles // 4)] + tot_b[...]
    loop(1, m, lambda k: tot_c_copy(k).start())
    for c in range(chunks):
        each(stage_c, c)

    def take_total(k, total):
        tot_c_copy(k).wait()
        return total + tot_c[k - 1]

    totals_row = gather(1, m, take_total, tot_b[quad * S_DEV // group])[0:1, :]
    spot = lax.rem(quad * S_DEV, group)
    lanes = lax.broadcasted_iota(jnp.int32, (S_DEV, group), 1)
    rows = lax.broadcasted_iota(jnp.int32, (S_DEV, group), 0)
    totals = jnp.sum(jnp.where(lanes == rows + spot, totals_row, 0.0), axis=1, keepdims=True)

    def g_copy(slot, to_slot, count, c, send_sem, recv_sem, dest):
        cols = pl.ds(c * wide, wide)
        return pltpu.make_async_remote_copy(
            src_ref=rows_g.at[pl.ds(slot, count), :, cols],
            dst_ref=rows_g.at[pl.ds(to_slot, count), :, cols],
            send_sem=send_sem,
            recv_sem=recv_sem,
            device_id={"blk": dest},
            device_id_type=MESH,
        )

    def line_copy(c, k):
        return g_copy(
            0, k, 1, c, line_send.at[c, k - 1], line_recv.at[c, k - 1], base + peer(k) * 4
        )

    def twin_copy(c, k):
        return g_copy(k, m + k, 1, c, twin_send.at[c, k], twin_recv.at[c, k], twin)

    def mate_copy(c, h):
        return g_copy(h * m, (2 + h) * m, m, c, mate_send.at[c, h], mate_recv.at[c, h], mate)

    for c in range(chunks):
        sums = []
        for p in range(c * per, (c + 1) * per):

            def take(k, total, p=p):
                c_copy(p, k).wait()
                return total + recv_c[p, k - 1].astype(F32)

            sums.append(gather(1, m, take, keep_c[p, quad]))
        pooled = jnp.concatenate(sums, axis=1) / (1.0 + totals)
        rows_g[0, :, c * wide : (c + 1) * wide] = pooled.astype(BF16)
        loop(1, m, lambda k, c=c: line_copy(c, k).start())
        twin_copy(c, 0).start()

    def on_line(c, k):
        line_copy(c, k).wait_recv()
        twin_copy(c, k).start()

    for c in range(chunks):
        loop(1, m, lambda k, c=c: on_line(c, k))
        mate_copy(c, 0).start()

    def normed_rows(low, count):
        block = rows_g[pl.ds(low, count)].reshape(count * S_DEV, width)
        wider = block.astype(F32)
        return block, lax.rsqrt(jnp.mean(wider * wider, axis=-1, keepdims=True) + 1e-06)

    proj_copy.wait()
    mine, scale = normed_rows(0, 1)
    queries = (jnp.dot(mine, proj[:, :width], preferred_element_type=F32) * scale).astype(BF16)
    queries = queries * jnp.asarray((width // HEADS) ** -0.5, BF16)

    def project(low, count):
        block, scale = normed_rows(low, count)
        keyval[pl.ds(low * S_DEV, count * S_DEV), :] = (
            jnp.dot(block, proj[:, width:], preferred_element_type=F32) * scale
        ).astype(BF16)

    def single_copy(c, k):
        return g_copy(m + k, 3 * m + k, 1, c, single_send.at[k], single_recv.at[k], mate)

    def pass_on(c, k):
        twin_copy(c, k).wait_recv()
        single_copy(c, k).start()

    def take_twin(c):
        if c < chunks - 1:
            loop(0, m, lambda k: twin_copy(c, k).wait_recv())
            mate_copy(c, 1).start()
        else:
            loop(0, m, lambda k: pass_on(c, k))

    project(0, m)
    for c in range(chunks - 1):
        take_twin(c)
    for c in range(chunks):
        mate_copy(c, 0).wait_recv()
    project(2 * m, m)
    take_twin(chunks - 1)
    project(m, m)
    for c in range(chunks - 1):
        mate_copy(c, 1).wait_recv()
    part = (chunks - 1) * wide if lastly.shape[0] == m * S_DEV else 0
    if part:
        lastly[...] = jnp.dot(
            rows_g[pl.ds(3 * m, m), :, :part].reshape(m * S_DEV, part),
            proj[:part, width:],
            preferred_element_type=F32,
        )
    loop(0, m, lambda k: single_copy(chunks - 1, k).wait_recv())
    if part:
        block, scale = normed_rows(3 * m, m)
        keyval[pl.ds(3 * m * S_DEV, m * S_DEV), :] = (
            (
                lastly[...]
                + jnp.dot(block[:, part:], proj[part:, width:], preferred_element_type=F32)
            )
            * scale
        ).astype(BF16)
    else:
        project(3 * m, m)

    head = width // HEADS
    pack = 256 // head
    span = pack * head
    column_head = lax.broadcasted_iota(jnp.int32, (S_DEV, span), 1) // head

    def score(g):
        block = queries[:, g * span : (g + 1) * span]
        stacked = jnp.concatenate(
            [jnp.where(column_head == h, block, jnp.zeros_like(block)) for h in range(pack)], axis=0
        )
        return lax.dot_general(
            stacked,
            keyval[:, pl.ds(g * span, span)],
            (((1,), (1,)), ((), ())),
            preferred_element_type=F32,
        )

    def mix(g, exps):
        values = keyval[:, pl.ds(width + g * span, span)]
        return jnp.dot(exps.astype(BF16), values, preferred_element_type=F32)

    groups = list(range(HEADS // pack))
    outs = []
    for batch in [groups] if n * S_DEV <= 1024 else [[g] for g in groups]:
        scores = [score(g) for g in batch]
        exps = [jnp.exp(row - jnp.max(row, axis=-1, keepdims=True)) for row in scores]
        mixes = [mix(g, some) for g, some in zip(batch, exps)]
        for mixed, some in zip(mixes, exps):
            mixed = mixed / jnp.sum(some, axis=-1, keepdims=True)
            piece = mixed[:S_DEV]
            for h in range(1, pack):
                piece = jnp.where(column_head == h, mixed[h * S_DEV : (h + 1) * S_DEV], piece)
            outs.append(piece)
    attended = jnp.concatenate(outs, axis=1)
    out_ref[...] = (rms_rows(attended) * gain_ref[...].astype(F32)[None, :]).astype(BF16)

    for c in range(pieces):
        a_copy(c).wait_send()
        b_copy(c).wait_send()
    for c in range(chunks):
        loop(1, m, lambda k, c=c: line_copy(c, k).wait_send())
        loop(0, m, lambda k, c=c: twin_copy(c, k).wait_send())
        mate_copy(c, 0).wait_send()
        if c < chunks - 1:
            mate_copy(c, 1).wait_send()
    loop(0, m, lambda k: single_copy(chunks - 1, k).wait_send())


def body(
    points_in,
    hidden_weight,
    output_weight,
    point_owner,
    point_node,
    point_weight,
    proj_weight,
    final_gain,
):
    n = lax.axis_size("blk")
    points, width = points_in.shape
    inner = hidden_weight.shape[1]
    m = n // 4
    chunks = 3 if width % (3 * 256) == 0 else 1
    parts = 5 if inner % (5 * 256) == 0 else 1
    nodes = n * S_DEV
    keep_type = F32 if nodes <= 1024 else BF16
    vmem = pl.BlockSpec(memory_space=pltpu.VMEM)
    hbm = pl.BlockSpec(memory_space=pl.ANY)
    dma = pltpu.SemaphoreType.DMA
    pieces = width // 128
    normed = pl.pallas_call(
        functools.partial(kernel, n),
        out_shape=jax.ShapeDtypeStruct((S_DEV, width), BF16),
        in_specs=[hbm] * 8,
        out_specs=vmem,
        scratch_shapes=[
            pltpu.VMEM((1, points), jnp.int32),
            pltpu.VMEM((1, points), jnp.int32),
            pltpu.VMEM((1, points), jnp.int32),
            pltpu.VMEM((width,), BF16),
            pltpu.VMEM((points, width), BF16),
            pltpu.VMEM(hidden_weight.shape, BF16),
            pltpu.VMEM(output_weight.shape, BF16),
            pltpu.VMEM(proj_weight.shape, BF16),
            pltpu.VMEM((points, width), BF16),
            pltpu.VMEM((points, inner), BF16),
            pltpu.VMEM((nodes, points), BF16),
            pltpu.VMEM((chunks, points, width // chunks), BF16),
            pltpu.VMEM((nodes // 128, 8, 128), F32),
            pltpu.VMEM((nodes // 256, 8, 128), F32),
            pltpu.VMEM((nodes // 512, 8, 128), F32),
            pltpu.VMEM((m - 1, 8, 128), F32),
            pltpu.VMEM((pieces, nodes // 2, 128), BF16),
            pltpu.VMEM((pieces, nodes // 2, 128), BF16),
            pltpu.VMEM((pieces, nodes // 2, 128), keep_type),
            pltpu.VMEM((pieces, nodes // 4, 128), BF16),
            pltpu.VMEM((pieces, nodes // 4, 128), BF16),
            pltpu.VMEM((pieces, nodes // 4, 128), F32),
            pltpu.VMEM((m, pieces, S_DEV, 128), BF16),
            pltpu.VMEM((pieces, m - 1, S_DEV, 128), BF16),
            pltpu.VMEM((pieces, m, S_DEV, 128), F32),
            pltpu.VMEM((n, S_DEV, width), BF16),
            pltpu.VMEM((nodes, 2 * width), BF16),
            pltpu.VMEM((m * S_DEV if nodes <= 1024 else 8, 2 * width), F32),
            dma((4,)),
            dma,
            dma((parts,)),
            dma((chunks,)),
            dma,
            dma((2,)),
            dma((2,)),
            dma((m - 1,)),
            dma((m - 1,)),
            dma((pieces,)),
            dma((pieces,)),
            dma((pieces,)),
            dma((pieces,)),
            dma((pieces, m - 1)),
            dma((pieces, m - 1)),
            dma((chunks, m - 1)),
            dma((chunks, m - 1)),
            dma((chunks, m)),
            dma((chunks, m)),
            dma((chunks, 2)),
            dma((chunks, 2)),
            dma((m,)),
            dma((m,)),
        ],
        compiler_params=pltpu.CompilerParams(
            collective_id=0, has_side_effects=True, vmem_limit_bytes=40_000_000 if nodes <= 1024 else 66_000_000
        ),
    )(
        *(
            pltpu.with_memory_space_constraint(x, pltpu.HBM)
            for x in (
                point_owner.reshape(1, points),
                point_node.reshape(1, points),
                point_weight.reshape(1, points),
                final_gain,
                points_in,
                hidden_weight,
                output_weight,
                proj_weight,
            )
        )
    )
    return normed


def solution(mesh):
    placed = (
        P(("groups", "blk"), None),
        P(),
        P(),
        P(("groups", "blk"), None),
        P(("groups", "blk")),
        P(("groups", "blk")),
        P(),
        P(),
    )
    return jax.shard_map(
        body, mesh=mesh, in_specs=placed, out_specs=P(("groups", "blk"), None), check_vma=False
    )
```

```python
import functools

import jax
import jax.numpy as jnp
from jax import lax
from jax.experimental import pallas as pl
from jax.experimental.pallas import tpu as pltpu
from jax.sharding import PartitionSpec as P

HEADS = 12
S_DEV = 32
MESH = pl.DeviceIdType.MESH
F32, BF16 = jnp.float32, jnp.bfloat16


def rms_rows(values):
    return values * lax.rsqrt(jnp.mean(values * values, axis=-1, keepdims=True) + 1e-06)


def gelu(values):
    return values * (0.5 + 0.5 * lax.erf(values * 0.7071067811865476))


def kernel(
    n,
    owner_hbm,
    node_hbm,
    weight_hbm,
    gain_hbm,
    points_hbm,
    w1_hbm,
    w2_hbm,
    proj_hbm,
    out_ref,
    owner_ref,
    node_ref,
    weight_ref,
    gain_ref,
    points_ref,
    w1,
    w2,
    proj,
    normed,
    hidden,
    coeffs,
    feats,
    tot,
    tot_a,
    tot_b,
    tot_c,
    send_a,
    recv_a,
    keep_a,
    send_b,
    recv_b,
    keep_b,
    send_c,
    recv_c,
    keep_c,
    rows_g,
    keyval,
    lastly,
    small_sem,
    points_sem,
    w1_sem,
    w2_sem,
    proj_sem,
    tot_send,
    tot_recv,
    totc_send,
    totc_recv,
    a_send,
    a_recv,
    b_send,
    b_recv,
    c_send,
    c_recv,
    line_send,
    line_recv,
    twin_send,
    twin_recv,
    mate_send,
    mate_recv,
    single_send,
    single_recv,
):
    me = lax.axis_index("blk")
    points, width = points_ref.shape
    parts = w1_sem.shape[0]
    part = w1.shape[1] // parts
    chunks = w2_sem.shape[0]
    wide = width // chunks
    pieces = send_a.shape[0]
    lane = send_a.shape[2]
    per = pieces // chunks
    m = n // 4
    bit0, bit1, quad = lax.rem(me, 2), lax.rem(me // 2, 2), me // 4
    mate = me + 1 - 2 * bit0
    twin = me + 2 - 4 * bit1
    base = me - quad * 4

    barrier = pltpu.get_barrier_semaphore()

    def greet(k, _):
        pl.semaphore_signal(
            barrier, inc=1, device_id={"blk": lax.rem(me + k, n)}, device_id_type=MESH
        )
        return 0


    w1_copies = [
        pltpu.make_async_copy(
            w1_hbm.at[:, pl.ds(i * part, part)], w1.at[:, pl.ds(i * part, part)], w1_sem.at[i]
        )
        for i in range(parts)
    ]
    w2_copies = [
        pltpu.make_async_copy(
            w2_hbm.at[:, pl.ds(i * wide, wide)], w2.at[:, pl.ds(i * wide, wide)], w2_sem.at[i]
        )
        for i in range(chunks)
    ]
    proj_copy = pltpu.make_async_copy(proj_hbm, proj, proj_sem)
    points_copy = pltpu.make_async_copy(points_hbm, points_ref, points_sem)
    small_copies = [
        pltpu.make_async_copy(source, dest, small_sem.at[i])
        for i, (source, dest) in enumerate(
            (
                (owner_hbm, owner_ref),
                (node_hbm, node_ref),
                (weight_hbm, weight_ref),
                (gain_hbm, gain_ref),
            )
        )
    ]
    points_copy.start()
    for copy in small_copies:
        copy.start()
    for copy in w1_copies[:3]:
        copy.start()
    lax.fori_loop(1, n, greet, 0)
    for copy in small_copies:
        copy.wait()

    owner = owner_ref[...]
    rel0 = lax.rem(owner + bit0, 2)
    rel1 = lax.rem(owner // 2 + bit1, 2)
    place = ((rel0 * 2 + rel1) * m + owner // 4) * S_DEV + node_ref[...]
    weights = weight_ref[...].astype(F32)
    group = 128
    for start in range(0, n * S_DEV, group):
        ids = start + lax.broadcasted_iota(jnp.int32, (group, points), 0)
        coeffs[pl.ds(start, group), :] = jnp.where(ids == place, weights, 0.0).astype(BF16)
        tot[start // group] = lax.dot_general(
            jnp.ones((8, points), BF16),
            coeffs[pl.ds(start, group), :],
            (((1,), (1,)), ((), ())),
            preferred_element_type=F32,
        )

    points_copy.wait()
    for copy in w1_copies[3:]:
        copy.start()
    normed[...] = rms_rows(points_ref[...].astype(F32)).astype(BF16)

    for i in range(parts):
        if i == 0:
            for copy in w1_copies[:2]:
                copy.wait()
            for copy in w2_copies:
                copy.start()
        if i == 2:
            for copy in w1_copies[2:]:
                copy.wait()
        cols = pl.ds(i * part, part)
        up = jnp.dot(normed[...], w1[:, cols], preferred_element_type=F32)
        hidden[:, cols] = gelu(up).astype(BF16)

    proj_copy.start()
    pl.semaphore_wait(barrier, n - 1)

    def loop(low, high, act):
        if high - low <= 4:
            for k in range(low, high):
                act(k)
            return

        def run(k, _):
            act(k)
            return 0

        lax.fori_loop(low, high, run, 0)

    def gather(low, high, act, total):
        if high - low <= 4:
            for k in range(low, high):
                total = act(k, total)
            return total
        return lax.fori_loop(low, high, act, total)

    def peer(k):
        if m != 4:
            return lax.rem(quad + k, m)
        return (quad + 1 - 2 * lax.rem(quad, 2), quad + 2 - 4 * (quad // 2), 3 - quad)[k - 1]

    tiles = tot.shape[0]

    def tot_a_copy():
        return pltpu.make_async_remote_copy(
            src_ref=tot.at[pl.ds(tiles // 2, tiles // 2)],
            dst_ref=tot_a,
            send_sem=tot_send.at[0],
            recv_sem=tot_recv.at[0],
            device_id={"blk": mate},
            device_id_type=MESH,
        )

    def tot_b_copy():
        return pltpu.make_async_remote_copy(
            src_ref=tot_a.at[pl.ds(tiles // 4, tiles // 4)],
            dst_ref=tot_b,
            send_sem=tot_send.at[1],
            recv_sem=tot_recv.at[1],
            device_id={"blk": twin},
            device_id_type=MESH,
        )

    def tot_c_copy(k):
        dest = peer(k)
        return pltpu.make_async_remote_copy(
            src_ref=tot_b.at[dest * S_DEV // group],
            dst_ref=tot_c.at[k - 1],
            send_sem=totc_send.at[k - 1],
            recv_sem=totc_recv.at[k - 1],
            device_id={"blk": base + dest * 4},
            device_id_type=MESH,
        )

    def a_copy(c):
        return pltpu.make_async_remote_copy(
            src_ref=send_a.at[c],
            dst_ref=recv_a.at[c],
            send_sem=a_send.at[c],
            recv_sem=a_recv.at[c],
            device_id={"blk": mate},
            device_id_type=MESH,
        )

    def b_copy(c):
        return pltpu.make_async_remote_copy(
            src_ref=send_b.at[c],
            dst_ref=recv_b.at[c],
            send_sem=b_send.at[c],
            recv_sem=b_recv.at[c],
            device_id={"blk": twin},
            device_id_type=MESH,
        )

    def c_copy(c, k):
        dest = peer(k)
        return pltpu.make_async_remote_copy(
            src_ref=send_c.at[dest, c],
            dst_ref=recv_c.at[c, k - 1],
            send_sem=c_send.at[c, k - 1],
            recv_sem=c_recv.at[c, k - 1],
            device_id={"blk": base + dest * 4},
            device_id_type=MESH,
        )

    half, quarter = n // 2 * S_DEV, m * S_DEV

    def features_of(c):
        if c == 0:
            for copy in w2_copies:
                copy.wait()
        cols = pl.ds(c * wide, wide)
        block = points // 4
        for r in range(4):
            rows = pl.ds(r * block, block)
            down = jnp.dot(hidden[rows, :], w2[:, cols], preferred_element_type=F32)
            feats[c, rows] = (points_ref[rows, cols].astype(F32) + down).astype(BF16)

    def stage_a(c):
        far = jnp.dot(coeffs[pl.ds(half, half), :], feats[c], preferred_element_type=F32)
        for j in range(per):
            send_a[c * per + j] = far[:, j * lane : (j + 1) * lane].astype(BF16)
            a_copy(c * per + j).start()
        near = jnp.dot(coeffs[pl.ds(0, half), :], feats[c], preferred_element_type=F32)
        for j in range(per):
            keep_a[c * per + j] = near[:, j * lane : (j + 1) * lane].astype(keep_a.dtype)

    def stage_b(p):
        a_copy(p).wait_recv()
        far = pl.ds(quarter, quarter)
        near = pl.ds(0, quarter)
        send_b[p] = (keep_a[p, far].astype(F32) + recv_a[p, far].astype(F32)).astype(BF16)
        b_copy(p).start()
        keep_b[p] = keep_a[p, near].astype(F32) + recv_a[p, near].astype(F32)

    def stage_c(p):
        b_copy(p).wait_recv()
        total = (keep_b[p] + recv_b[p].astype(F32)).reshape(m, S_DEV, lane)
        keep_c[p] = total
        for q in range(m):
            send_c[q, p] = total[q].astype(BF16)

        loop(1, m, lambda k: c_copy(p, k).start())

    def each(stage, c):
        if 0 <= c < chunks:
            for p in range(c * per, (c + 1) * per):
                stage(p)

    tot_a_copy().start()
    for c in range(chunks):
        features_of(c)
        if c == 1:
            tot_a_copy().wait()
            tot_a[...] = tot[pl.ds(0, tiles // 2)] + tot_a[...]
            tot_b_copy().start()
        each(stage_b, c - 1)
        stage_a(c)
    if chunks == 1:
        tot_a_copy().wait()
        tot_a[...] = tot[pl.ds(0, tiles // 2)] + tot_a[...]
        tot_b_copy().start()
    each(stage_b, chunks - 1)
    tot_b_copy().wait()
    tot_b[...] = tot_a[pl.ds(0, tiles // 4)] + tot_b[...]
    loop(1, m, lambda k: tot_c_copy(k).start())
    for c in range(chunks):
        each(stage_c, c)

    def take_total(k, total):
        tot_c_copy(k).wait()
        return total + tot_c[k - 1]

    totals_row = gather(1, m, take_total, tot_b[quad * S_DEV // group])[0:1, :]
    spot = lax.rem(quad * S_DEV, group)
    lanes = lax.broadcasted_iota(jnp.int32, (S_DEV, group), 1)
    rows = lax.broadcasted_iota(jnp.int32, (S_DEV, group), 0)
    totals = jnp.sum(jnp.where(lanes == rows + spot, totals_row, 0.0), axis=1, keepdims=True)

    def g_copy(slot, to_slot, count, c, send_sem, recv_sem, dest):
        cols = pl.ds(c * wide, wide)
        return pltpu.make_async_remote_copy(
            src_ref=rows_g.at[pl.ds(slot, count), :, cols],
            dst_ref=rows_g.at[pl.ds(to_slot, count), :, cols],
            send_sem=send_sem,
            recv_sem=recv_sem,
            device_id={"blk": dest},
            device_id_type=MESH,
        )

    def line_copy(c, k):
        return g_copy(
            0, k, 1, c, line_send.at[c, k - 1], line_recv.at[c, k - 1], base + peer(k) * 4
        )

    def twin_copy(c, k):
        return g_copy(k, m + k, 1, c, twin_send.at[c, k], twin_recv.at[c, k], twin)

    def mate_copy(c, h):
        return g_copy(h * m, (2 + h) * m, m, c, mate_send.at[c, h], mate_recv.at[c, h], mate)

    for c in range(chunks):
        sums = []
        for p in range(c * per, (c + 1) * per):

            def take(k, total, p=p):
                c_copy(p, k).wait_recv()
                return total + recv_c[p, k - 1].astype(F32)

            sums.append(gather(1, m, take, keep_c[p, quad]))
        pooled = jnp.concatenate(sums, axis=1) / (1.0 + totals)
        rows_g[0, :, c * wide : (c + 1) * wide] = pooled.astype(BF16)
        loop(1, m, lambda k, c=c: line_copy(c, k).start())
        twin_copy(c, 0).start()

    def on_line(c, k):
        line_copy(c, k).wait_recv()
        twin_copy(c, k).start()

    for c in range(chunks):
        loop(1, m, lambda k, c=c: on_line(c, k))
        mate_copy(c, 0).start()

    def normed_rows(low, count):
        block = rows_g[pl.ds(low, count)].reshape(count * S_DEV, width)
        wider = block.astype(F32)
        return block, lax.rsqrt(jnp.mean(wider * wider, axis=-1, keepdims=True) + 1e-06)

    proj_copy.wait()
    mine, scale = normed_rows(0, 1)
    queries = (jnp.dot(mine, proj[:, :width], preferred_element_type=F32) * scale).astype(BF16)
    queries = queries * jnp.asarray((width // HEADS) ** -0.5, BF16)

    def project(low, count):
        block, scale = normed_rows(low, count)
        keyval[pl.ds(low * S_DEV, count * S_DEV), :] = (
            jnp.dot(block, proj[:, width:], preferred_element_type=F32) * scale
        ).astype(BF16)

    def single_copy(c, k):
        return g_copy(m + k, 3 * m + k, 1, c, single_send.at[k], single_recv.at[k], mate)

    def pass_on(c, k):
        twin_copy(c, k).wait_recv()
        single_copy(c, k).start()

    def take_twin(c):
        if c < chunks - 1:
            loop(0, m, lambda k: twin_copy(c, k).wait_recv())
            mate_copy(c, 1).start()
        else:
            loop(0, m, lambda k: pass_on(c, k))

    project(0, m)
    for c in range(chunks - 1):
        take_twin(c)
    for c in range(chunks):
        mate_copy(c, 0).wait_recv()
    project(2 * m, m)
    for p in range(pieces):
        a_copy(p).wait_send()
        b_copy(p).wait_send()
        loop(1, m, lambda k, p=p: c_copy(p, k).wait_send())
    for c in range(chunks):
        loop(1, m, lambda k, c=c: line_copy(c, k).wait_send())
        mate_copy(c, 0).wait_send()
    take_twin(chunks - 1)
    project(m, m)
    for c in range(chunks):
        loop(0, m, lambda k, c=c: twin_copy(c, k).wait_send())
        if c < chunks - 1:
            mate_copy(c, 1).wait_send()
    for c in range(chunks - 1):
        mate_copy(c, 1).wait_recv()
    part = (chunks - 1) * wide if lastly.shape[0] == m * S_DEV else 0
    if part:
        lastly[...] = jnp.dot(
            rows_g[pl.ds(3 * m, m), :, :part].reshape(m * S_DEV, part),
            proj[:part, width:],
            preferred_element_type=F32,
        )
    loop(0, m, lambda k: single_copy(chunks - 1, k).wait())
    if part:
        block, scale = normed_rows(3 * m, m)
        keyval[pl.ds(3 * m * S_DEV, m * S_DEV), :] = (
            (
                lastly[...]
                + jnp.dot(block[:, part:], proj[part:, width:], preferred_element_type=F32)
            )
            * scale
        ).astype(BF16)
    else:
        project(3 * m, m)

    head = width // HEADS
    pack = 256 // head
    span = pack * head
    column_head = lax.broadcasted_iota(jnp.int32, (S_DEV, span), 1) // head

    def score(g):
        block = queries[:, g * span : (g + 1) * span]
        stacked = jnp.concatenate(
            [jnp.where(column_head == h, block, jnp.zeros_like(block)) for h in range(pack)], axis=0
        )
        return lax.dot_general(
            stacked,
            keyval[:, pl.ds(g * span, span)],
            (((1,), (1,)), ((), ())),
            preferred_element_type=F32,
        )

    def mix(g, exps):
        values = keyval[:, pl.ds(width + g * span, span)]
        return jnp.dot(exps.astype(BF16), values, preferred_element_type=F32)

    groups = list(range(HEADS // pack))
    outs = []
    for batch in [groups] if n * S_DEV <= 1024 else [[g] for g in groups]:
        scores = [score(g) for g in batch]
        exps = [jnp.exp(row - jnp.max(row, axis=-1, keepdims=True)) for row in scores]
        mixes = [mix(g, some) for g, some in zip(batch, exps)]
        for mixed, some in zip(mixes, exps):
            mixed = mixed / jnp.sum(some, axis=-1, keepdims=True)
            piece = mixed[:S_DEV]
            for h in range(1, pack):
                piece = jnp.where(column_head == h, mixed[h * S_DEV : (h + 1) * S_DEV], piece)
            outs.append(piece)
    attended = jnp.concatenate(outs, axis=1)
    out_ref[...] = (rms_rows(attended) * gain_ref[...].astype(F32)[None, :]).astype(BF16)


def body(
    points_in,
    hidden_weight,
    output_weight,
    point_owner,
    point_node,
    point_weight,
    proj_weight,
    final_gain,
):
    n = lax.axis_size("blk")
    points, width = points_in.shape
    inner = hidden_weight.shape[1]
    m = n // 4
    chunks = 3 if width % (3 * 256) == 0 else 1
    parts = 5 if inner % (5 * 256) == 0 else 1
    nodes = n * S_DEV
    keep_type = F32 if nodes <= 1024 else BF16
    vmem = pl.BlockSpec(memory_space=pltpu.VMEM)
    hbm = pl.BlockSpec(memory_space=pl.ANY)
    dma = pltpu.SemaphoreType.DMA
    pieces = width // 128
    normed = pl.pallas_call(
        functools.partial(kernel, n),
        out_shape=jax.ShapeDtypeStruct((S_DEV, width), BF16),
        in_specs=[hbm] * 8,
        out_specs=vmem,
        scratch_shapes=[
            pltpu.VMEM((1, points), jnp.int32),
            pltpu.VMEM((1, points), jnp.int32),
            pltpu.VMEM((1, points), jnp.int32),
            pltpu.VMEM((width,), BF16),
            pltpu.VMEM((points, width), BF16),
            pltpu.VMEM(hidden_weight.shape, BF16),
            pltpu.VMEM(output_weight.shape, BF16),
            pltpu.VMEM(proj_weight.shape, BF16),
            pltpu.VMEM((points, width), BF16),
            pltpu.VMEM((points, inner), BF16),
            pltpu.VMEM((nodes, points), BF16),
            pltpu.VMEM((chunks, points, width // chunks), BF16),
            pltpu.VMEM((nodes // 128, 8, 128), F32),
            pltpu.VMEM((nodes // 256, 8, 128), F32),
            pltpu.VMEM((nodes // 512, 8, 128), F32),
            pltpu.VMEM((m - 1, 8, 128), F32),
            pltpu.VMEM((pieces, nodes // 2, 128), BF16),
            pltpu.VMEM((pieces, nodes // 2, 128), BF16),
            pltpu.VMEM((pieces, nodes // 2, 128), keep_type),
            pltpu.VMEM((pieces, nodes // 4, 128), BF16),
            pltpu.VMEM((pieces, nodes // 4, 128), BF16),
            pltpu.VMEM((pieces, nodes // 4, 128), F32),
            pltpu.VMEM((m, pieces, S_DEV, 128), BF16),
            pltpu.VMEM((pieces, m - 1, S_DEV, 128), BF16),
            pltpu.VMEM((pieces, m, S_DEV, 128), F32),
            pltpu.VMEM((n, S_DEV, width), BF16),
            pltpu.VMEM((nodes, 2 * width), BF16),
            pltpu.VMEM((m * S_DEV if nodes <= 1024 else 8, 2 * width), F32),
            dma((4,)),
            dma,
            dma((parts,)),
            dma((chunks,)),
            dma,
            dma((2,)),
            dma((2,)),
            dma((m - 1,)),
            dma((m - 1,)),
            dma((pieces,)),
            dma((pieces,)),
            dma((pieces,)),
            dma((pieces,)),
            dma((pieces, m - 1)),
            dma((pieces, m - 1)),
            dma((chunks, m - 1)),
            dma((chunks, m - 1)),
            dma((chunks, m)),
            dma((chunks, m)),
            dma((chunks, 2)),
            dma((chunks, 2)),
            dma((m,)),
            dma((m,)),
        ],
        compiler_params=pltpu.CompilerParams(
            collective_id=0, has_side_effects=True, vmem_limit_bytes=40_000_000 if nodes <= 1024 else 66_000_000
        ),
    )(
        *(
            pltpu.with_memory_space_constraint(x, pltpu.HBM)
            for x in (
                point_owner.reshape(1, points),
                point_node.reshape(1, points),
                point_weight.reshape(1, points),
                final_gain,
                points_in,
                hidden_weight,
                output_weight,
                proj_weight,
            )
        )
    )
    return normed


def solution(mesh):
    placed = (
        P(("groups", "blk"), None),
        P(),
        P(),
        P(("groups", "blk"), None),
        P(("groups", "blk")),
        P(("groups", "blk")),
        P(),
        P(),
    )
    return jax.shard_map(
        body, mesh=mesh, in_specs=placed, out_specs=P(("groups", "blk"), None), check_vma=False
    )
```

```python
import functools

import jax
import jax.numpy as jnp
from jax import lax
from jax.experimental import pallas as pl
from jax.experimental.pallas import tpu as pltpu
from jax.sharding import PartitionSpec as P

HEADS = 12
S_DEV = 32
MESH = pl.DeviceIdType.MESH
F32, BF16 = jnp.float32, jnp.bfloat16


def rms_rows(values):
    return values * lax.rsqrt(jnp.mean(values * values, axis=-1, keepdims=True) + 1e-06)


def gelu(values):
    return values * (0.5 + 0.5 * lax.erf(values * 0.7071067811865476))


def kernel(
    n,
    owner_hbm,
    node_hbm,
    weight_hbm,
    gain_hbm,
    points_hbm,
    w1_hbm,
    w2_hbm,
    proj_hbm,
    out_ref,
    owner_ref,
    node_ref,
    weight_ref,
    gain_ref,
    points_ref,
    w1,
    w2,
    proj,
    normed,
    hidden,
    coeffs,
    feats,
    tot,
    tot_a,
    tot_b,
    tot_c,
    send_a,
    recv_a,
    keep_a,
    send_b,
    recv_b,
    keep_b,
    send_c,
    recv_c,
    keep_c,
    rows_g,
    keyval,
    lastly,
    small_sem,
    points_sem,
    w1_sem,
    w2_sem,
    proj_sem,
    tot_send,
    tot_recv,
    totc_send,
    totc_recv,
    a_send,
    a_recv,
    b_send,
    b_recv,
    c_send,
    c_recv,
    line_send,
    line_recv,
    twin_send,
    twin_recv,
    mate_send,
    mate_recv,
    single_send,
    single_recv,
):
    me = lax.axis_index("blk")
    points, width = points_ref.shape
    parts = w1_sem.shape[0]
    part = w1.shape[1] // parts
    chunks = w2_sem.shape[0]
    wide = width // chunks
    pieces = send_a.shape[0]
    lane = send_a.shape[2]
    per = pieces // chunks
    m = n // 4
    bit0, bit1, quad = lax.rem(me, 2), lax.rem(me // 2, 2), me // 4
    mate = me + 1 - 2 * bit0
    twin = me + 2 - 4 * bit1
    base = me - quad * 4

    barrier = pltpu.get_barrier_semaphore()

    def greet(k, _):
        pl.semaphore_signal(
            barrier, inc=1, device_id={"blk": lax.rem(me + k, n)}, device_id_type=MESH
        )
        return 0


    w1_copies = [
        pltpu.make_async_copy(
            w1_hbm.at[:, pl.ds(i * part, part)], w1.at[:, pl.ds(i * part, part)], w1_sem.at[i]
        )
        for i in range(parts)
    ]
    w2_copies = [
        pltpu.make_async_copy(
            w2_hbm.at[:, pl.ds(i * wide, wide)], w2.at[:, pl.ds(i * wide, wide)], w2_sem.at[i]
        )
        for i in range(chunks)
    ]
    proj_copy = pltpu.make_async_copy(proj_hbm, proj, proj_sem)
    points_copy = pltpu.make_async_copy(points_hbm, points_ref, points_sem)
    small_copies = [
        pltpu.make_async_copy(source, dest, small_sem.at[i])
        for i, (source, dest) in enumerate(
            (
                (owner_hbm, owner_ref),
                (node_hbm, node_ref),
                (weight_hbm, weight_ref),
                (gain_hbm, gain_ref),
            )
        )
    ]
    points_copy.start()
    for copy in small_copies:
        copy.start()
    for copy in w1_copies[:3]:
        copy.start()
    lax.fori_loop(1, n, greet, 0)
    for copy in small_copies:
        copy.wait()

    owner = owner_ref[...]
    rel0 = lax.rem(owner + bit0, 2)
    rel1 = lax.rem(owner // 2 + bit1, 2)
    place = ((rel0 * 2 + rel1) * m + owner // 4) * S_DEV + node_ref[...]
    weights = weight_ref[...].astype(F32)
    group = 128
    for start in range(0, n * S_DEV, group):
        ids = start + lax.broadcasted_iota(jnp.int32, (group, points), 0)
        coeffs[pl.ds(start, group), :] = jnp.where(ids == place, weights, 0.0).astype(BF16)
        tot[start // group] = lax.dot_general(
            jnp.ones((8, points), BF16),
            coeffs[pl.ds(start, group), :],
            (((1,), (1,)), ((), ())),
            preferred_element_type=F32,
        )

    points_copy.wait()
    for copy in w1_copies[3:]:
        copy.start()
    normed[...] = rms_rows(points_ref[...].astype(F32)).astype(BF16)

    for i in range(parts):
        if i == 0:
            for copy in w1_copies[:2]:
                copy.wait()
            for copy in w2_copies:
                copy.start()
        if i == 2:
            for copy in w1_copies[2:]:
                copy.wait()
        cols = pl.ds(i * part, part)
        up = jnp.dot(normed[...], w1[:, cols], preferred_element_type=F32)
        hidden[:, cols] = gelu(up).astype(BF16)

    proj_copy.start()
    pl.semaphore_wait(barrier, n - 1)

    def loop(low, high, act):
        if high - low <= 4:
            for k in range(low, high):
                act(k)
            return

        def run(k, _):
            act(k)
            return 0

        lax.fori_loop(low, high, run, 0)

    def gather(low, high, act, total):
        if high - low <= 4:
            for k in range(low, high):
                total = act(k, total)
            return total
        return lax.fori_loop(low, high, act, total)

    def peer(k):
        if m != 4:
            return lax.rem(quad + k, m)
        return (quad + 1 - 2 * lax.rem(quad, 2), quad + 2 - 4 * (quad // 2), 3 - quad)[k - 1]

    tiles = tot.shape[0]

    def tot_a_copy():
        return pltpu.make_async_remote_copy(
            src_ref=tot.at[pl.ds(tiles // 2, tiles // 2)],
            dst_ref=tot_a,
            send_sem=tot_send.at[0],
            recv_sem=tot_recv.at[0],
            device_id={"blk": mate},
            device_id_type=MESH,
        )

    def tot_b_copy():
        return pltpu.make_async_remote_copy(
            src_ref=tot_a.at[pl.ds(tiles // 4, tiles // 4)],
            dst_ref=tot_b,
            send_sem=tot_send.at[1],
            recv_sem=tot_recv.at[1],
            device_id={"blk": twin},
            device_id_type=MESH,
        )

    def tot_c_copy(k):
        dest = peer(k)
        return pltpu.make_async_remote_copy(
            src_ref=tot_b.at[dest * S_DEV // group],
            dst_ref=tot_c.at[k - 1],
            send_sem=totc_send.at[k - 1],
            recv_sem=totc_recv.at[k - 1],
            device_id={"blk": base + dest * 4},
            device_id_type=MESH,
        )

    def a_copy(c):
        return pltpu.make_async_remote_copy(
            src_ref=send_a.at[c],
            dst_ref=recv_a.at[c],
            send_sem=a_send.at[c],
            recv_sem=a_recv.at[c],
            device_id={"blk": mate},
            device_id_type=MESH,
        )

    def b_copy(c):
        return pltpu.make_async_remote_copy(
            src_ref=send_b.at[c],
            dst_ref=recv_b.at[c],
            send_sem=b_send.at[c],
            recv_sem=b_recv.at[c],
            device_id={"blk": twin},
            device_id_type=MESH,
        )

    def c_copy(c, k):
        dest = peer(k)
        return pltpu.make_async_remote_copy(
            src_ref=send_c.at[dest, c],
            dst_ref=recv_c.at[c, k - 1],
            send_sem=c_send.at[c, k - 1],
            recv_sem=c_recv.at[c, k - 1],
            device_id={"blk": base + dest * 4},
            device_id_type=MESH,
        )

    half, quarter = n // 2 * S_DEV, m * S_DEV

    def features_of(c):
        if c == 0:
            for copy in w2_copies:
                copy.wait()
        cols = pl.ds(c * wide, wide)
        block = points // 4
        for r in range(4):
            rows = pl.ds(r * block, block)
            down = jnp.dot(hidden[rows, :], w2[:, cols], preferred_element_type=F32)
            feats[c, rows] = (points_ref[rows, cols].astype(F32) + down).astype(BF16)

    def stage_a(c):
        far = jnp.dot(coeffs[pl.ds(half, half), :], feats[c], preferred_element_type=F32)
        for j in range(per):
            send_a[c * per + j] = far[:, j * lane : (j + 1) * lane].astype(BF16)
            a_copy(c * per + j).start()
        near = jnp.dot(coeffs[pl.ds(0, half), :], feats[c], preferred_element_type=F32)
        for j in range(per):
            keep_a[c * per + j] = near[:, j * lane : (j + 1) * lane].astype(keep_a.dtype)

    def stage_b(p):
        a_copy(p).wait_recv()
        far = pl.ds(quarter, quarter)
        near = pl.ds(0, quarter)
        send_b[p] = (keep_a[p, far].astype(F32) + recv_a[p, far].astype(F32)).astype(BF16)
        b_copy(p).start()
        keep_b[p] = keep_a[p, near].astype(F32) + recv_a[p, near].astype(F32)

    def stage_c(p):
        b_copy(p).wait_recv()
        total = (keep_b[p] + recv_b[p].astype(F32)).reshape(m, S_DEV, lane)
        keep_c[p] = total
        for q in range(m):
            send_c[q, p] = total[q].astype(BF16)

        loop(1, m, lambda k: c_copy(p, k).start())

    def each(stage, c):
        if 0 <= c < chunks:
            for p in range(c * per, (c + 1) * per):
                stage(p)

    tot_a_copy().start()
    for c in range(chunks):
        features_of(c)
        if c == 1:
            tot_a_copy().wait()
            tot_a[...] = tot[pl.ds(0, tiles // 2)] + tot_a[...]
            tot_b_copy().start()
        each(stage_b, c - 1)
        stage_a(c)
    if chunks == 1:
        tot_a_copy().wait()
        tot_a[...] = tot[pl.ds(0, tiles // 2)] + tot_a[...]
        tot_b_copy().start()
    each(stage_b, chunks - 1)
    tot_b_copy().wait()
    tot_b[...] = tot_a[pl.ds(0, tiles // 4)] + tot_b[...]
    loop(1, m, lambda k: tot_c_copy(k).start())
    for c in range(chunks):
        each(stage_c, c)

    def take_total(k, total):
        tot_c_copy(k).wait()
        return total + tot_c[k - 1]

    totals_row = gather(1, m, take_total, tot_b[quad * S_DEV // group])[0:1, :]
    spot = lax.rem(quad * S_DEV, group)
    lanes = lax.broadcasted_iota(jnp.int32, (S_DEV, group), 1)
    rows = lax.broadcasted_iota(jnp.int32, (S_DEV, group), 0)
    totals = jnp.sum(jnp.where(lanes == rows + spot, totals_row, 0.0), axis=1, keepdims=True)

    def g_copy(slot, to_slot, count, c, send_sem, recv_sem, dest):
        cols = pl.ds(c * wide, wide)
        return pltpu.make_async_remote_copy(
            src_ref=rows_g.at[pl.ds(slot, count), :, cols],
            dst_ref=rows_g.at[pl.ds(to_slot, count), :, cols],
            send_sem=send_sem,
            recv_sem=recv_sem,
            device_id={"blk": dest},
            device_id_type=MESH,
        )

    def line_copy(c, k):
        return g_copy(
            0, k, 1, c, line_send.at[c, k - 1], line_recv.at[c, k - 1], base + peer(k) * 4
        )

    def twin_copy(c, k):
        return g_copy(k, m + k, 1, c, twin_send.at[c, k], twin_recv.at[c, k], twin)

    def mate_copy(c, h):
        return g_copy(h * m, (2 + h) * m, m, c, mate_send.at[c, h], mate_recv.at[c, h], mate)

    for c in range(chunks):
        sums = []
        for p in range(c * per, (c + 1) * per):

            def take(k, total, p=p):
                c_copy(p, k).wait_recv()
                return total + recv_c[p, k - 1].astype(F32)

            sums.append(gather(1, m, take, keep_c[p, quad]))
        pooled = jnp.concatenate(sums, axis=1) / (1.0 + totals)
        rows_g[0, :, c * wide : (c + 1) * wide] = pooled.astype(BF16)
        twin_copy(c, 0).start()
        loop(1, m, lambda k, c=c: line_copy(c, k).start())

    def on_line(c, k):
        line_copy(c, k).wait_recv()
        twin_copy(c, k).start()

    for c in range(chunks):
        loop(1, m, lambda k, c=c: on_line(c, k))
        mate_copy(c, 0).start()

    def normed_rows(low, count):
        block = rows_g[pl.ds(low, count)].reshape(count * S_DEV, width)
        wider = block.astype(F32)
        return block, lax.rsqrt(jnp.mean(wider * wider, axis=-1, keepdims=True) + 1e-06)

    proj_copy.wait()
    mine, scale = normed_rows(0, 1)
    queries = (jnp.dot(mine, proj[:, :width], preferred_element_type=F32) * scale).astype(BF16)
    queries = queries * jnp.asarray((width // HEADS) ** -0.5, BF16)

    def project(low, count):
        block, scale = normed_rows(low, count)
        keyval[pl.ds(low * S_DEV, count * S_DEV), :] = (
            jnp.dot(block, proj[:, width:], preferred_element_type=F32) * scale
        ).astype(BF16)

    def single_copy(c, k):
        return g_copy(m + k, 3 * m + k, 1, c, single_send.at[k], single_recv.at[k], mate)

    def pass_on(c, k):
        twin_copy(c, k).wait_recv()
        single_copy(c, k).start()

    def take_twin(c):
        if c < chunks - 1:
            loop(0, m, lambda k: twin_copy(c, k).wait_recv())
            mate_copy(c, 1).start()
        else:
            loop(0, m, lambda k: pass_on(c, k))

    project(0, m)
    for c in range(chunks - 1):
        take_twin(c)
    for c in range(chunks):
        mate_copy(c, 0).wait_recv()
    project(2 * m, m)
    for p in range(pieces):
        a_copy(p).wait_send()
        b_copy(p).wait_send()
        loop(1, m, lambda k, p=p: c_copy(p, k).wait_send())
    for c in range(chunks):
        loop(1, m, lambda k, c=c: line_copy(c, k).wait_send())
        mate_copy(c, 0).wait_send()
    take_twin(chunks - 1)
    project(m, m)
    for c in range(chunks):
        loop(0, m, lambda k, c=c: twin_copy(c, k).wait_send())
        if c < chunks - 1:
            mate_copy(c, 1).wait_send()
    for c in range(chunks - 1):
        mate_copy(c, 1).wait_recv()
    part = (chunks - 1) * wide if lastly.shape[0] == m * S_DEV else 0
    if part:
        lastly[...] = jnp.dot(
            rows_g[pl.ds(3 * m, m), :, :part].reshape(m * S_DEV, part),
            proj[:part, width:],
            preferred_element_type=F32,
        )
    loop(0, m, lambda k: single_copy(chunks - 1, k).wait())
    if part:
        block, scale = normed_rows(3 * m, m)
        keyval[pl.ds(3 * m * S_DEV, m * S_DEV), :] = (
            (
                lastly[...]
                + jnp.dot(block[:, part:], proj[part:, width:], preferred_element_type=F32)
            )
            * scale
        ).astype(BF16)
    else:
        project(3 * m, m)

    head = width // HEADS
    pack = 256 // head
    span = pack * head
    column_head = lax.broadcasted_iota(jnp.int32, (S_DEV, span), 1) // head

    def score(g):
        block = queries[:, g * span : (g + 1) * span]
        stacked = jnp.concatenate(
            [jnp.where(column_head == h, block, jnp.zeros_like(block)) for h in range(pack)], axis=0
        )
        return lax.dot_general(
            stacked,
            keyval[:, pl.ds(g * span, span)],
            (((1,), (1,)), ((), ())),
            preferred_element_type=F32,
        )

    def mix(g, exps):
        values = keyval[:, pl.ds(width + g * span, span)]
        return jnp.dot(exps.astype(BF16), values, preferred_element_type=F32)

    groups = list(range(HEADS // pack))
    outs = []
    for batch in [groups] if n * S_DEV <= 1024 else [[g] for g in groups]:
        scores = [score(g) for g in batch]
        exps = [jnp.exp(row - jnp.max(row, axis=-1, keepdims=True)) for row in scores]
        mixes = [mix(g, some) for g, some in zip(batch, exps)]
        for mixed, some in zip(mixes, exps):
            mixed = mixed / jnp.sum(some, axis=-1, keepdims=True)
            piece = mixed[:S_DEV]
            for h in range(1, pack):
                piece = jnp.where(column_head == h, mixed[h * S_DEV : (h + 1) * S_DEV], piece)
            outs.append(piece)
    attended = jnp.concatenate(outs, axis=1)
    out_ref[...] = (rms_rows(attended) * gain_ref[...].astype(F32)[None, :]).astype(BF16)


def body(
    points_in,
    hidden_weight,
    output_weight,
    point_owner,
    point_node,
    point_weight,
    proj_weight,
    final_gain,
):
    n = lax.axis_size("blk")
    points, width = points_in.shape
    inner = hidden_weight.shape[1]
    m = n // 4
    chunks = 3 if width % (3 * 256) == 0 else 1
    parts = 5 if inner % (5 * 256) == 0 else 1
    nodes = n * S_DEV
    keep_type = F32 if nodes <= 1024 else BF16
    vmem = pl.BlockSpec(memory_space=pltpu.VMEM)
    hbm = pl.BlockSpec(memory_space=pl.ANY)
    dma = pltpu.SemaphoreType.DMA
    pieces = width // 128
    normed = pl.pallas_call(
        functools.partial(kernel, n),
        out_shape=jax.ShapeDtypeStruct((S_DEV, width), BF16),
        in_specs=[hbm] * 8,
        out_specs=vmem,
        scratch_shapes=[
            pltpu.VMEM((1, points), jnp.int32),
            pltpu.VMEM((1, points), jnp.int32),
            pltpu.VMEM((1, points), jnp.int32),
            pltpu.VMEM((width,), BF16),
            pltpu.VMEM((points, width), BF16),
            pltpu.VMEM(hidden_weight.shape, BF16),
            pltpu.VMEM(output_weight.shape, BF16),
            pltpu.VMEM(proj_weight.shape, BF16),
            pltpu.VMEM((points, width), BF16),
            pltpu.VMEM((points, inner), BF16),
            pltpu.VMEM((nodes, points), BF16),
            pltpu.VMEM((chunks, points, width // chunks), BF16),
            pltpu.VMEM((nodes // 128, 8, 128), F32),
            pltpu.VMEM((nodes // 256, 8, 128), F32),
            pltpu.VMEM((nodes // 512, 8, 128), F32),
            pltpu.VMEM((m - 1, 8, 128), F32),
            pltpu.VMEM((pieces, nodes // 2, 128), BF16),
            pltpu.VMEM((pieces, nodes // 2, 128), BF16),
            pltpu.VMEM((pieces, nodes // 2, 128), keep_type),
            pltpu.VMEM((pieces, nodes // 4, 128), BF16),
            pltpu.VMEM((pieces, nodes // 4, 128), BF16),
            pltpu.VMEM((pieces, nodes // 4, 128), F32),
            pltpu.VMEM((m, pieces, S_DEV, 128), BF16),
            pltpu.VMEM((pieces, m - 1, S_DEV, 128), BF16),
            pltpu.VMEM((pieces, m, S_DEV, 128), F32),
            pltpu.VMEM((n, S_DEV, width), BF16),
            pltpu.VMEM((nodes, 2 * width), BF16),
            pltpu.VMEM((m * S_DEV if nodes <= 1024 else 8, 2 * width), F32),
            dma((4,)),
            dma,
            dma((parts,)),
            dma((chunks,)),
            dma,
            dma((2,)),
            dma((2,)),
            dma((m - 1,)),
            dma((m - 1,)),
            dma((pieces,)),
            dma((pieces,)),
            dma((pieces,)),
            dma((pieces,)),
            dma((pieces, m - 1)),
            dma((pieces, m - 1)),
            dma((chunks, m - 1)),
            dma((chunks, m - 1)),
            dma((chunks, m)),
            dma((chunks, m)),
            dma((chunks, 2)),
            dma((chunks, 2)),
            dma((m,)),
            dma((m,)),
        ],
        compiler_params=pltpu.CompilerParams(
            collective_id=0, has_side_effects=True, vmem_limit_bytes=40_000_000 if nodes <= 1024 else 66_000_000
        ),
    )(
        *(
            pltpu.with_memory_space_constraint(x, pltpu.HBM)
            for x in (
                point_owner.reshape(1, points),
                point_node.reshape(1, points),
                point_weight.reshape(1, points),
                final_gain,
                points_in,
                hidden_weight,
                output_weight,
                proj_weight,
            )
        )
    )
    return normed


def solution(mesh):
    placed = (
        P(("groups", "blk"), None),
        P(),
        P(),
        P(("groups", "blk"), None),
        P(("groups", "blk")),
        P(("groups", "blk")),
        P(),
        P(),
    )
    return jax.shard_map(
        body, mesh=mesh, in_specs=placed, out_specs=P(("groups", "blk"), None), check_vma=False
    )
```

```python
import functools

import jax
import jax.numpy as jnp
from jax import lax
from jax.experimental import pallas as pl
from jax.experimental.pallas import tpu as pltpu
from jax.sharding import PartitionSpec as P

HEADS = 12
S_DEV = 32
MESH = pl.DeviceIdType.MESH
F32, BF16 = jnp.float32, jnp.bfloat16


def rms_rows(values):
    return values * lax.rsqrt(jnp.mean(values * values, axis=-1, keepdims=True) + 1e-06)


def gelu(values):
    return values * (0.5 + 0.5 * lax.erf(values * 0.7071067811865476))


def kernel(
    n,
    owner_hbm,
    node_hbm,
    weight_hbm,
    gain_hbm,
    points_hbm,
    w1_hbm,
    w2_hbm,
    proj_hbm,
    out_ref,
    owner_ref,
    node_ref,
    weight_ref,
    gain_ref,
    points_ref,
    w1,
    w2,
    proj,
    normed,
    hidden,
    coeffs,
    feats,
    tot,
    tot_a,
    tot_b,
    tot_c,
    send_a,
    recv_a,
    keep_a,
    send_b,
    recv_b,
    keep_b,
    send_c,
    recv_c,
    keep_c,
    rows_g,
    keyval,
    lastly,
    small_sem,
    points_sem,
    w1_sem,
    w2_sem,
    proj_sem,
    tot_send,
    tot_recv,
    totc_send,
    totc_recv,
    a_send,
    a_recv,
    b_send,
    b_recv,
    c_send,
    c_recv,
    line_send,
    line_recv,
    twin_send,
    twin_recv,
    mate_send,
    mate_recv,
    single_send,
    single_recv,
):
    me = lax.axis_index("blk")
    points, width = points_ref.shape
    parts = w1_sem.shape[0]
    part = w1.shape[1] // parts
    chunks = w2_sem.shape[0]
    wide = width // chunks
    pieces = send_a.shape[0]
    lane = send_a.shape[2]
    per = pieces // chunks
    m = n // 4
    bit0, bit1, quad = lax.rem(me, 2), lax.rem(me // 2, 2), me // 4
    mate = me + 1 - 2 * bit0
    twin = me + 2 - 4 * bit1
    base = me - quad * 4

    barrier = pltpu.get_barrier_semaphore()

    def greet(k, _):
        pl.semaphore_signal(
            barrier, inc=1, device_id={"blk": lax.rem(me + k, n)}, device_id_type=MESH
        )
        return 0


    w1_copies = [
        pltpu.make_async_copy(
            w1_hbm.at[:, pl.ds(i * part, part)], w1.at[:, pl.ds(i * part, part)], w1_sem.at[i]
        )
        for i in range(parts)
    ]
    w2_copies = [
        pltpu.make_async_copy(
            w2_hbm.at[:, pl.ds(i * wide, wide)], w2.at[:, pl.ds(i * wide, wide)], w2_sem.at[i]
        )
        for i in range(chunks)
    ]
    proj_copy = pltpu.make_async_copy(proj_hbm, proj, proj_sem)
    points_copy = pltpu.make_async_copy(points_hbm, points_ref, points_sem)
    small_copies = [
        pltpu.make_async_copy(source, dest, small_sem.at[i])
        for i, (source, dest) in enumerate(
            (
                (owner_hbm, owner_ref),
                (node_hbm, node_ref),
                (weight_hbm, weight_ref),
                (gain_hbm, gain_ref),
            )
        )
    ]
    points_copy.start()
    for copy in small_copies:
        copy.start()
    for copy in w1_copies[:3]:
        copy.start()
    lax.fori_loop(1, n, greet, 0)
    for copy in small_copies:
        copy.wait()

    owner = owner_ref[...]
    rel0 = lax.rem(owner + bit0, 2)
    rel1 = lax.rem(owner // 2 + bit1, 2)
    place = ((rel0 * 2 + rel1) * m + owner // 4) * S_DEV + node_ref[...]
    weights = weight_ref[...].astype(F32)
    group = 128
    for start in range(0, n * S_DEV, group):
        ids = start + lax.broadcasted_iota(jnp.int32, (group, points), 0)
        coeffs[pl.ds(start, group), :] = jnp.where(ids == place, weights, 0.0).astype(BF16)
        tot[start // group] = lax.dot_general(
            jnp.ones((8, points), BF16),
            coeffs[pl.ds(start, group), :],
            (((1,), (1,)), ((), ())),
            preferred_element_type=F32,
        )

    points_copy.wait()
    for copy in w1_copies[3:]:
        copy.start()
    normed[...] = rms_rows(points_ref[...].astype(F32)).astype(BF16)

    for i in range(parts):
        if i == 0:
            for copy in w1_copies[:2]:
                copy.wait()
            for copy in w2_copies:
                copy.start()
        if i == 2:
            for copy in w1_copies[2:]:
                copy.wait()
        cols = pl.ds(i * part, part)
        up = jnp.dot(normed[...], w1[:, cols], preferred_element_type=F32)
        hidden[:, cols] = gelu(up).astype(BF16)

    proj_copy.start()
    pl.semaphore_wait(barrier, n - 1)

    def loop(low, high, act):
        if high - low <= 4:
            for k in range(low, high):
                act(k)
            return

        def run(k, _):
            act(k)
            return 0

        lax.fori_loop(low, high, run, 0)

    def gather(low, high, act, total):
        if high - low <= 4:
            for k in range(low, high):
                total = act(k, total)
            return total
        return lax.fori_loop(low, high, act, total)

    def peer(k):
        if m != 4:
            return lax.rem(quad + k, m)
        return (quad + 1 - 2 * lax.rem(quad, 2), quad + 2 - 4 * (quad // 2), 3 - quad)[k - 1]

    tiles = tot.shape[0]

    def tot_a_copy():
        return pltpu.make_async_remote_copy(
            src_ref=tot.at[pl.ds(tiles // 2, tiles // 2)],
            dst_ref=tot_a,
            send_sem=tot_send.at[0],
            recv_sem=tot_recv.at[0],
            device_id={"blk": mate},
            device_id_type=MESH,
        )

    def tot_b_copy():
        return pltpu.make_async_remote_copy(
            src_ref=tot_a.at[pl.ds(tiles // 4, tiles // 4)],
            dst_ref=tot_b,
            send_sem=tot_send.at[1],
            recv_sem=tot_recv.at[1],
            device_id={"blk": twin},
            device_id_type=MESH,
        )

    def tot_c_copy(k):
        dest = peer(k)
        return pltpu.make_async_remote_copy(
            src_ref=tot_b.at[dest * S_DEV // group],
            dst_ref=tot_c.at[k - 1],
            send_sem=totc_send.at[k - 1],
            recv_sem=totc_recv.at[k - 1],
            device_id={"blk": base + dest * 4},
            device_id_type=MESH,
        )

    def a_copy(c):
        return pltpu.make_async_remote_copy(
            src_ref=send_a.at[c],
            dst_ref=recv_a.at[c],
            send_sem=a_send.at[c],
            recv_sem=a_recv.at[c],
            device_id={"blk": mate},
            device_id_type=MESH,
        )

    def b_copy(c):
        return pltpu.make_async_remote_copy(
            src_ref=send_b.at[c],
            dst_ref=recv_b.at[c],
            send_sem=b_send.at[c],
            recv_sem=b_recv.at[c],
            device_id={"blk": twin},
            device_id_type=MESH,
        )

    def c_copy(c, k):
        dest = peer(k)
        return pltpu.make_async_remote_copy(
            src_ref=send_c.at[dest, c],
            dst_ref=recv_c.at[c, k - 1],
            send_sem=c_send.at[c, k - 1],
            recv_sem=c_recv.at[c, k - 1],
            device_id={"blk": base + dest * 4},
            device_id_type=MESH,
        )

    half, quarter = n // 2 * S_DEV, m * S_DEV

    def features_of(c):
        if c == 0:
            for copy in w2_copies:
                copy.wait()
        cols = pl.ds(c * wide, wide)
        block = points // 4
        for r in range(4):
            rows = pl.ds(r * block, block)
            down = jnp.dot(hidden[rows, :], w2[:, cols], preferred_element_type=F32)
            feats[c, rows] = (points_ref[rows, cols].astype(F32) + down).astype(BF16)

    def stage_a(c):
        far = jnp.dot(coeffs[pl.ds(half, half), :], feats[c], preferred_element_type=F32)
        for j in range(per):
            send_a[c * per + j] = far[:, j * lane : (j + 1) * lane].astype(BF16)
            a_copy(c * per + j).start()
        near = jnp.dot(coeffs[pl.ds(0, half), :], feats[c], preferred_element_type=F32)
        for j in range(per):
            keep_a[c * per + j] = near[:, j * lane : (j + 1) * lane].astype(keep_a.dtype)

    def stage_b(p):
        a_copy(p).wait_recv()
        far = pl.ds(quarter, quarter)
        near = pl.ds(0, quarter)
        send_b[p] = (keep_a[p, far].astype(F32) + recv_a[p, far].astype(F32)).astype(BF16)
        b_copy(p).start()
        keep_b[p] = keep_a[p, near].astype(F32) + recv_a[p, near].astype(F32)

    def stage_c(p):
        b_copy(p).wait_recv()
        total = (keep_b[p] + recv_b[p].astype(F32)).reshape(m, S_DEV, lane)
        keep_c[p] = total
        for q in range(m):
            send_c[q, p] = total[q].astype(BF16)

        loop(1, m, lambda k: c_copy(p, m - k).start())

    def each(stage, c):
        if 0 <= c < chunks:
            for p in range(c * per, (c + 1) * per):
                stage(p)

    tot_a_copy().start()
    for c in range(chunks):
        features_of(c)
        if c == 1:
            tot_a_copy().wait()
            tot_a[...] = tot[pl.ds(0, tiles // 2)] + tot_a[...]
            tot_b_copy().start()
        each(stage_b, c - 1)
        stage_a(c)
    if chunks == 1:
        tot_a_copy().wait()
        tot_a[...] = tot[pl.ds(0, tiles // 2)] + tot_a[...]
        tot_b_copy().start()
    each(stage_b, chunks - 1)
    tot_b_copy().wait()
    tot_b[...] = tot_a[pl.ds(0, tiles // 4)] + tot_b[...]
    loop(1, m, lambda k: tot_c_copy(k).start())
    for c in range(chunks):
        each(stage_c, c)

    def take_total(k, total):
        tot_c_copy(k).wait()
        return total + tot_c[k - 1]

    totals_row = gather(1, m, take_total, tot_b[quad * S_DEV // group])[0:1, :]
    spot = lax.rem(quad * S_DEV, group)
    lanes = lax.broadcasted_iota(jnp.int32, (S_DEV, group), 1)
    rows = lax.broadcasted_iota(jnp.int32, (S_DEV, group), 0)
    totals = jnp.sum(jnp.where(lanes == rows + spot, totals_row, 0.0), axis=1, keepdims=True)

    def g_copy(slot, to_slot, count, c, send_sem, recv_sem, dest):
        cols = pl.ds(c * wide, wide)
        return pltpu.make_async_remote_copy(
            src_ref=rows_g.at[pl.ds(slot, count), :, cols],
            dst_ref=rows_g.at[pl.ds(to_slot, count), :, cols],
            send_sem=send_sem,
            recv_sem=recv_sem,
            device_id={"blk": dest},
            device_id_type=MESH,
        )

    def line_copy(c, k):
        return g_copy(
            0, k, 1, c, line_send.at[c, k - 1], line_recv.at[c, k - 1], base + peer(k) * 4
        )

    def twin_copy(c, k):
        return g_copy(k, m + k, 1, c, twin_send.at[c, k], twin_recv.at[c, k], twin)

    def mate_copy(c, h):
        return g_copy(h * m, (2 + h) * m, m, c, mate_send.at[c, h], mate_recv.at[c, h], mate)

    for c in range(chunks):
        sums = []
        for p in range(c * per, (c + 1) * per):

            def take(k, total, p=p):
                c_copy(p, k).wait_recv()
                return total + recv_c[p, k - 1].astype(F32)

            sums.append(gather(1, m, take, keep_c[p, quad]))
        pooled = jnp.concatenate(sums, axis=1) / (1.0 + totals)
        rows_g[0, :, c * wide : (c + 1) * wide] = pooled.astype(BF16)
        twin_copy(c, 0).start()
        loop(1, m, lambda k, c=c: line_copy(c, k).start())

    def on_line(c, k):
        line_copy(c, k).wait_recv()
        twin_copy(c, k).start()

    for c in range(chunks):
        loop(1, m, lambda k, c=c: on_line(c, k))
        mate_copy(c, 0).start()

    def normed_rows(low, count):
        block = rows_g[pl.ds(low, count)].reshape(count * S_DEV, width)
        wider = block.astype(F32)
        return block, lax.rsqrt(jnp.mean(wider * wider, axis=-1, keepdims=True) + 1e-06)

    proj_copy.wait()
    mine, scale = normed_rows(0, 1)
    queries = (jnp.dot(mine, proj[:, :width], preferred_element_type=F32) * scale).astype(BF16)
    queries = queries * jnp.asarray((width // HEADS) ** -0.5, BF16)

    def project(low, count):
        block, scale = normed_rows(low, count)
        keyval[pl.ds(low * S_DEV, count * S_DEV), :] = (
            jnp.dot(block, proj[:, width:], preferred_element_type=F32) * scale
        ).astype(BF16)

    def single_copy(c, k):
        return g_copy(m + k, 3 * m + k, 1, c, single_send.at[k], single_recv.at[k], mate)

    def pass_on(c, k):
        twin_copy(c, k).wait_recv()
        single_copy(c, k).start()

    def take_twin(c):
        if c < chunks - 1:
            loop(0, m, lambda k: twin_copy(c, k).wait_recv())
            mate_copy(c, 1).start()
        else:
            loop(0, m, lambda k: pass_on(c, k))

    project(0, m)
    for c in range(chunks - 1):
        take_twin(c)
    for c in range(chunks):
        mate_copy(c, 0).wait_recv()
    project(2 * m, m)
    for p in range(pieces):
        a_copy(p).wait_send()
        b_copy(p).wait_send()
        loop(1, m, lambda k, p=p: c_copy(p, k).wait_send())
    for c in range(chunks):
        loop(1, m, lambda k, c=c: line_copy(c, k).wait_send())
        mate_copy(c, 0).wait_send()
    take_twin(chunks - 1)
    project(m, m)
    for c in range(chunks):
        loop(0, m, lambda k, c=c: twin_copy(c, k).wait_send())
        if c < chunks - 1:
            mate_copy(c, 1).wait_send()
    for c in range(chunks - 1):
        mate_copy(c, 1).wait_recv()
    part = (chunks - 1) * wide if lastly.shape[0] == m * S_DEV else 0
    if part:
        lastly[...] = jnp.dot(
            rows_g[pl.ds(3 * m, m), :, :part].reshape(m * S_DEV, part),
            proj[:part, width:],
            preferred_element_type=F32,
        )
    loop(0, m, lambda k: single_copy(chunks - 1, k).wait())
    if part:
        block, scale = normed_rows(3 * m, m)
        keyval[pl.ds(3 * m * S_DEV, m * S_DEV), :] = (
            (
                lastly[...]
                + jnp.dot(block[:, part:], proj[part:, width:], preferred_element_type=F32)
            )
            * scale
        ).astype(BF16)
    else:
        project(3 * m, m)

    head = width // HEADS
    pack = 256 // head
    span = pack * head
    column_head = lax.broadcasted_iota(jnp.int32, (S_DEV, span), 1) // head

    def score(g):
        block = queries[:, g * span : (g + 1) * span]
        stacked = jnp.concatenate(
            [jnp.where(column_head == h, block, jnp.zeros_like(block)) for h in range(pack)], axis=0
        )
        return lax.dot_general(
            stacked,
            keyval[:, pl.ds(g * span, span)],
            (((1,), (1,)), ((), ())),
            preferred_element_type=F32,
        )

    def mix(g, exps):
        values = keyval[:, pl.ds(width + g * span, span)]
        return jnp.dot(exps.astype(BF16), values, preferred_element_type=F32)

    groups = list(range(HEADS // pack))
    outs = []
    for batch in [groups] if n * S_DEV <= 1024 else [[g] for g in groups]:
        scores = [score(g) for g in batch]
        exps = [jnp.exp(row - jnp.max(row, axis=-1, keepdims=True)) for row in scores]
        mixes = [mix(g, some) for g, some in zip(batch, exps)]
        for mixed, some in zip(mixes, exps):
            mixed = mixed / jnp.sum(some, axis=-1, keepdims=True)
            piece = mixed[:S_DEV]
            for h in range(1, pack):
                piece = jnp.where(column_head == h, mixed[h * S_DEV : (h + 1) * S_DEV], piece)
            outs.append(piece)
    attended = jnp.concatenate(outs, axis=1)
    out_ref[...] = (rms_rows(attended) * gain_ref[...].astype(F32)[None, :]).astype(BF16)


def body(
    points_in,
    hidden_weight,
    output_weight,
    point_owner,
    point_node,
    point_weight,
    proj_weight,
    final_gain,
):
    n = lax.axis_size("blk")
    points, width = points_in.shape
    inner = hidden_weight.shape[1]
    m = n // 4
    chunks = 3 if width % (3 * 256) == 0 else 1
    parts = 5 if inner % (5 * 256) == 0 else 1
    nodes = n * S_DEV
    keep_type = F32 if nodes <= 1024 else BF16
    vmem = pl.BlockSpec(memory_space=pltpu.VMEM)
    hbm = pl.BlockSpec(memory_space=pl.ANY)
    dma = pltpu.SemaphoreType.DMA
    pieces = width // 128
    normed = pl.pallas_call(
        functools.partial(kernel, n),
        out_shape=jax.ShapeDtypeStruct((S_DEV, width), BF16),
        in_specs=[hbm] * 8,
        out_specs=vmem,
        scratch_shapes=[
            pltpu.VMEM((1, points), jnp.int32),
            pltpu.VMEM((1, points), jnp.int32),
            pltpu.VMEM((1, points), jnp.int32),
            pltpu.VMEM((width,), BF16),
            pltpu.VMEM((points, width), BF16),
            pltpu.VMEM(hidden_weight.shape, BF16),
            pltpu.VMEM(output_weight.shape, BF16),
            pltpu.VMEM(proj_weight.shape, BF16),
            pltpu.VMEM((points, width), BF16),
            pltpu.VMEM((points, inner), BF16),
            pltpu.VMEM((nodes, points), BF16),
            pltpu.VMEM((chunks, points, width // chunks), BF16),
            pltpu.VMEM((nodes // 128, 8, 128), F32),
            pltpu.VMEM((nodes // 256, 8, 128), F32),
            pltpu.VMEM((nodes // 512, 8, 128), F32),
            pltpu.VMEM((m - 1, 8, 128), F32),
            pltpu.VMEM((pieces, nodes // 2, 128), BF16),
            pltpu.VMEM((pieces, nodes // 2, 128), BF16),
            pltpu.VMEM((pieces, nodes // 2, 128), keep_type),
            pltpu.VMEM((pieces, nodes // 4, 128), BF16),
            pltpu.VMEM((pieces, nodes // 4, 128), BF16),
            pltpu.VMEM((pieces, nodes // 4, 128), F32),
            pltpu.VMEM((m, pieces, S_DEV, 128), BF16),
            pltpu.VMEM((pieces, m - 1, S_DEV, 128), BF16),
            pltpu.VMEM((pieces, m, S_DEV, 128), F32),
            pltpu.VMEM((n, S_DEV, width), BF16),
            pltpu.VMEM((nodes, 2 * width), BF16),
            pltpu.VMEM((m * S_DEV if nodes <= 1024 else 8, 2 * width), F32),
            dma((4,)),
            dma,
            dma((parts,)),
            dma((chunks,)),
            dma,
            dma((2,)),
            dma((2,)),
            dma((m - 1,)),
            dma((m - 1,)),
            dma((pieces,)),
            dma((pieces,)),
            dma((pieces,)),
            dma((pieces,)),
            dma((pieces, m - 1)),
            dma((pieces, m - 1)),
            dma((chunks, m - 1)),
            dma((chunks, m - 1)),
            dma((chunks, m)),
            dma((chunks, m)),
            dma((chunks, 2)),
            dma((chunks, 2)),
            dma((m,)),
            dma((m,)),
        ],
        compiler_params=pltpu.CompilerParams(
            collective_id=0, has_side_effects=True, vmem_limit_bytes=40_000_000 if nodes <= 1024 else 66_000_000
        ),
    )(
        *(
            pltpu.with_memory_space_constraint(x, pltpu.HBM)
            for x in (
                point_owner.reshape(1, points),
                point_node.reshape(1, points),
                point_weight.reshape(1, points),
                final_gain,
                points_in,
                hidden_weight,
                output_weight,
                proj_weight,
            )
        )
    )
    return normed


def solution(mesh):
    placed = (
        P(("groups", "blk"), None),
        P(),
        P(),
        P(("groups", "blk"), None),
        P(("groups", "blk")),
        P(("groups", "blk")),
        P(),
        P(),
    )
    return jax.shard_map(
        body, mesh=mesh, in_specs=placed, out_specs=P(("groups", "blk"), None), check_vma=False
    )
```
